32 devices in a mesh: dp: 8 (over y, x, core), mp: 4 (over z).
Axes of the slice: x: 2, y: 2, z: 4, core: 2. Of those that a mesh axis runs over, the one named last changes fastest.
Arguments:
- inputs: bfloat16 [16, 1024, 2048], P('dp', 'mp'), may hold values from -6 to 6
- segment_ids: int32 [16, 1024], P('dp'), may hold values from 0 to 7, never falling along the last dimension, each value on 1 to 512 neighbouring positions
- cotangent: bfloat16 [16, 1024, 2048], P('dp', 'mp'), may hold values from -6 to 6
- query_weight: bfloat16 [2048, 2048], P('dp', 'mp'), may hold values from -0.125 to 0.125
- key_weight: bfloat16 [2048, 2048], P('dp', 'mp'), may hold values from -0.125 to 0.125
- value_weight: bfloat16 [2048, 2048], P('dp', 'mp'), may hold values from -0.125 to 0.125
- out_weight: bfloat16 [2048, 2048], P('mp', 'dp'), may hold values from -0.75 to 0.75
- up_weight: bfloat16 [2048, 8192], P('dp', 'mp'), may hold values from -0.125 to 0.125
- down_weight: bfloat16 [8192, 2048], P('mp', 'dp'), may hold values from -0.0625 to 0.0625
- query_bias: float32 [2048], replicated, may hold values from -3 to 3
- value_bias: float32 [2048], replicated, may hold values from -3 to 3
- out_bias: float32 [2048], replicated, may hold values from -2 to 2
- up_bias: float32 [8192], replicated, may hold values from -3 to 3
- down_bias: float32 [2048], replicated, may hold values from -2 to 2
- first_gain: float32 [2048], replicated, may hold values from 0.1 to 1.9
- first_shift: float32 [2048], replicated, may hold values from -2 to 2
- second_gain: float32 [2048], replicated, may hold values from 0.1 to 1.9
- second_shift: float32 [2048], replicated, may hold values from -2 to 2
Outputs:
- outputs: bfloat16 [16, 1024, 2048], P('dp', 'mp')
- grad_inputs: float32 [16, 1024, 2048], P('dp', 'mp')
- grad_query_weight: float32 [2048, 2048], P('dp', 'mp')
- grad_key_weight: float32 [2048, 2048], P('dp', 'mp')
- grad_value_weight: float32 [2048, 2048], P('dp', 'mp')
- grad_out_weight: float32 [2048, 2048], P('mp', 'dp')
- grad_up_weight: float32 [2048, 8192], P('dp', 'mp')
- grad_down_weight: float32 [8192, 2048], P('mp', 'dp')
- grad_query_bias: float32 [2048], replicated
- grad_value_bias: float32 [2048], replicated
- grad_out_bias: float32 [2048], replicated
- grad_up_bias: float32 [8192], replicated
- grad_down_bias: float32 [2048], replicated
- grad_first_gain: float32 [2048], replicated
- grad_first_shift: float32 [2048], replicated
- grad_second_gain: float32 [2048], replicated
- grad_second_shift: float32 [2048], replicated
The draws below stay inside these ranges and needn't reach their ends.
Inputs may be any that keep to these rules, and one draw needn't show every extreme that they name: `segment_ids`: along each sequence the numbers never fall; each document holds 1 to 512 tokens, and one of each sequence holds exactly 512.
All inputs are finite; a program needn't handle non-finite values.
Results may differ from the reference program's by a relative error of at most 0.014.
Values may be sent and summed in bfloat16 or wider, within the bound.
A program may use at most 320 MiB of HBM per device.

```python
import math
import jax
import jax.numpy as jnp
import numpy as np
from jax import lax

D = 2048
HEADS = 16
HEAD_DIM = 128
FF = 8192
LEN = 1024
SEQS = 16


def level_of(own_key, shape, cuts, smallest, top_value):
    gain, own = 1.0, jax.random.fold_in(own_key, 6)
    for axis_at, blocks in cuts:
        steps = jnp.exp(jax.random.uniform(jax.random.fold_in(own, axis_at), (blocks,), jnp.float32, smallest / len(cuts), top_value / len(cuts)))
        gain = gain * jnp.repeat(steps, shape[axis_at] // blocks).reshape([-1 if axis == axis_at else 1 for axis in range(len(shape))])
    return gain


def split_up(number_of, total, most, slope):
    loads = [(1 << 20) // math.isqrt(rank ** slope) + 1 for rank in range(2, number_of + 1)]
    surplus, holding = total - most - (number_of - 1), [1] * (number_of - 1)
    while surplus > 0:
        movable = [i for i in range(number_of - 1) if holding[i] < most]
        mass, remaining = sum([loads[i] for i in movable]), surplus
        for i in movable:
            more = min(most - holding[i], max(1, remaining * loads[i] // mass), surplus)
            holding[i] = holding[i] + more
            surplus = surplus - more
    return np.array([most] + holding)


def uneven_parts(key, number_of, total, bound, skew):
    if number_of == 2:
        one = jax.random.randint(key, (), max(1, total - bound), min(bound, total - 1) + 1)
        return jnp.stack([one, total - one])
    tallies = jnp.asarray(split_up(number_of, total, bound, skew), jnp.int32)
    couples = (number_of - 1) // 2
    giver, receiver = tallies[1:1 + 2 * couples:2], tallies[2:2 + 2 * couples:2]
    room = jnp.minimum(giver - 1, bound - receiver)
    moved = jax.random.randint(jax.random.fold_in(key, 1), (couples,), 0, 1 << 20) % (room + 1)
    tallies = tallies.at[1:1 + 2 * couples:2].set(giver - moved).at[2:2 + 2 * couples:2].set(receiver + moved)
    return tallies[jax.random.permutation(jax.random.fold_in(key, 2), number_of)]


def normal_values(own_key, dims, spread, most, shards=(), kind=jnp.bfloat16):
    level = level_of(own_key, dims, shards, -0.22, 0.18) if shards else 1.0
    result = jax.random.normal(own_key, dims, jnp.float32) * spread * level
    return jnp.minimum(jnp.maximum(result, -most), most).astype(kind)


def setup_inputs(seed: int = 0) -> dict:
    streams_of = jax.random.split(jax.random.key(seed), 19)
    return {
        "inputs": normal_values(streams_of[0], (SEQS, LEN, D), 1.0, 6.0, ((0, 8), (1, 4))),
        "segment_ids": jax.vmap(lambda own: jnp.searchsorted(jnp.cumsum(uneven_parts(own, 8, LEN, LEN // 2, 2)), jnp.arange(LEN), side="right"))(jax.random.split(streams_of[1], SEQS)).reshape((SEQS, LEN)).astype(jnp.int32),
        "cotangent": normal_values(streams_of[2], (SEQS, LEN, D), 1.0, 6.0, ((0, 8), (1, 4))),
        "query_weight": normal_values(streams_of[3], (D, D), D ** -0.5, 0.125, ((0, 8), (1, 4))),
        "key_weight": normal_values(streams_of[4], (D, D), D ** -0.5, 0.125, ((0, 8), (1, 4))),
        "value_weight": normal_values(streams_of[5], (D, D), D ** -0.5, 0.125, ((0, 8), (1, 4))),
        "out_weight": normal_values(streams_of[6], (D, D), (D // 32) ** -0.5, 0.75, ((0, 4), (1, 8))),
        "up_weight": normal_values(streams_of[7], (D, FF), D ** -0.5, 0.125, ((0, 8), (1, 4))),
        "down_weight": normal_values(streams_of[8], (FF, D), FF ** -0.5, 0.0625, ((0, 4), (1, 8))),
        "query_bias": normal_values(streams_of[9], (D,), 0.5, 3.0, (), jnp.float32),
        "value_bias": normal_values(streams_of[10], (D,), 0.5, 3.0, (), jnp.float32),
        "out_bias": normal_values(streams_of[11], (D,), 0.3, 2.0, (), jnp.float32),
        "up_bias": normal_values(streams_of[12], (FF,), 0.5, 3.0, (), jnp.float32),
        "down_bias": normal_values(streams_of[13], (D,), 0.3, 2.0, (), jnp.float32),
        "first_gain": jnp.clip(1.0 + 0.18 * jax.random.normal(streams_of[14], (D,), jnp.float32), 0.1, 1.9),
        "first_shift": normal_values(streams_of[15], (D,), 0.3, 2.0, (), jnp.float32),
        "second_gain": jnp.clip(1.0 + 0.18 * jax.random.normal(streams_of[16], (D,), jnp.float32), 0.1, 1.9),
        "second_shift": normal_values(streams_of[17], (D,), 0.3, 2.0, (), jnp.float32),
    }


EPSILON = 1e-12
masked_score = -1e+30
highest = lax.Precision.HIGHEST

@jax.custom_vjp
def low(v):
    return lax.optimization_barrier(v.astype(jnp.bfloat16)).astype(jnp.float32)

@jax.custom_vjp
def low_back(v):
    return v

def low_keep(v):
    return (low(v), None)

def low_pass(kept, grad):
    return (grad,)

def back_keep(v):
    return (v, None)

def back_low(kept, grad):
    return (low(grad),)
low.defvjp(low_keep, low_pass)
low_back.defvjp(back_keep, back_low)

def product(left, right):
    return jnp.dot(left, right, precision=highest, preferred_element_type=jnp.float32)

def layer_norm(resid, scale_vec, shift_vec):
    average = lax.optimization_barrier(jnp.mean(resid, axis=-1, keepdims=True))
    centered = resid - average
    variance = lax.optimization_barrier(jnp.mean(centered * centered, axis=-1, keepdims=True))
    return centered * lax.rsqrt(variance + EPSILON) * scale_vec + shift_vec

def layer_forward(tokens_in, params, segments):
    query_weight, key_weight, value_weight, out_weight, up_weight, down_weight, query_bias, value_bias, out_bias, up_bias, down_bias, first_gain, first_shift, second_gain, second_shift = params
    length = tokens_in.shape[0]
    queries = low(low_back(product(tokens_in, query_weight) + query_bias)).reshape(length, HEADS, HEAD_DIM)
    keys_all = low(low_back(product(tokens_in, key_weight))).reshape(length, HEADS, HEAD_DIM)
    values_all = low(low_back(product(tokens_in, value_weight) + value_bias)).reshape(length, HEADS, HEAD_DIM)
    logits = jnp.einsum('qhd,khd->hqk', queries, keys_all, precision=highest) * HEAD_DIM ** (-0.5)
    logits = low_back(logits)
    allowed = segments[:, None] == segments[None, :]
    logits = jnp.where(allowed[None], logits, masked_score)
    row_max = lax.optimization_barrier(jnp.max(logits, axis=-1, keepdims=True))
    expo_vals = jnp.exp(logits - row_max)
    probs = expo_vals / lax.optimization_barrier(jnp.sum(expo_vals, axis=-1, keepdims=True))
    attended = jnp.einsum('hqk,khd->qhd', low(probs), values_all, precision=highest).reshape(length, D)
    attended = low(low_back(attended))
    branch_attn = low_back(product(attended, out_weight) + out_bias)
    first_out = layer_norm(tokens_in + branch_attn, first_gain, first_shift)
    up_proj = low_back(product(low(first_out), up_weight) + up_bias)
    hidden = low(jax.nn.gelu(up_proj, approximate=True))
    branch_ffn = low_back(product(hidden, down_weight) + down_bias)
    return layer_norm(first_out + branch_ffn, second_gain, second_shift)

def reference(inputs, segment_ids, cotangent, query_weight, key_weight, value_weight, out_weight, up_weight, down_weight, query_bias, value_bias, out_bias, up_bias, down_bias, first_gain, first_shift, second_gain, second_shift):
    params = tuple((member.astype(jnp.float32) for member in (query_weight, key_weight, value_weight, out_weight, up_weight, down_weight, query_bias, value_bias, out_bias, up_bias, down_bias, first_gain, first_shift, second_gain, second_shift)))

    def one_sequence(totals, sequence):
        tokens_in, segments, tangent = sequence
        outcome, backward = jax.vjp(lambda values_in, params_in: layer_forward(values_in, params_in, segments), tokens_in.astype(jnp.float32), params)
        grad_in, grad_params = backward(tangent.astype(jnp.float32))
        totals = jax.tree.map(jnp.add, totals, grad_params)
        return (totals, (outcome.astype(jnp.bfloat16), grad_in))
    zeros_init = jax.tree.map(jnp.zeros_like, params)
    totals, (outputs, grad_inputs) = lax.scan(one_sequence, zeros_init, (inputs, segment_ids, cotangent))
    return (outputs, grad_inputs, totals[0], totals[1], totals[2], totals[3], totals[4], totals[5], totals[6], totals[7], totals[8], totals[9], totals[10], totals[11], totals[12], totals[13], totals[14])
```

```python
import functools

import jax
import jax.numpy as jnp
from jax import lax
from jax.experimental import pallas as pl
from jax.experimental.pallas import tpu as pltpu
from jax.sharding import PartitionSpec as P

HEAD_DIM = 128
SCALING = HEAD_DIM ** (-0.5)
EPSILON = 1e-12
MASKED = -1e30
LOW = jnp.bfloat16
WIDE = jnp.float32


def contract(left, right, left_dim, right_dim):
    return lax.dot_general(
        left, right, (((left_dim,), (right_dim,)), ((), ())), preferred_element_type=WIDE
    )


def norm_forward(resid, scale_vec, shift_vec):
    average = jnp.mean(resid, axis=-1, keepdims=True)
    centered = resid - average
    variance = jnp.mean(centered * centered, axis=-1, keepdims=True)
    inv_std = lax.rsqrt(variance + EPSILON)
    normed = centered * inv_std
    return normed * scale_vec + shift_vec, normed, inv_std


def norm_backward(upstream, normed, inv_std, scale_vec):
    scaled = upstream * scale_vec
    first_mean = jnp.mean(scaled, axis=-1, keepdims=True)
    second_mean = jnp.mean(scaled * normed, axis=-1, keepdims=True)
    return inv_std * (scaled - first_mean - normed * second_mean)


def gelu_tanh(values_in):
    return jax.nn.gelu(values_in, approximate=True)


def head_rows(refs, column):
    return jnp.concatenate([ref[:, column : column + HEAD_DIM] for ref in refs], axis=0)


def forward_kernel(heads, parts, which, *refs):
    qkv_refs = refs[:parts]
    keys_segment, query_segments, out_ref, lse_ref = refs[parts:]
    segment_col = keys_segment[0]
    segment_row = query_segments[0, which : which + 1]
    allowed = segment_col == segment_row
    for head in range(heads):
        queries = qkv_refs[which][:, head * HEAD_DIM : (head + 1) * HEAD_DIM]
        keys_all = head_rows(qkv_refs, (heads + head) * HEAD_DIM)
        values_all = head_rows(qkv_refs, (2 * heads + head) * HEAD_DIM)
        logits = jnp.where(allowed, contract(keys_all, queries, 1, 1) * SCALING, MASKED)
        top = jnp.max(logits, axis=0, keepdims=True)
        expo = jnp.exp(logits - top)
        total = jnp.sum(expo, axis=0, keepdims=True)
        probs_low = (expo * (1.0 / total)).astype(LOW)
        mixed = contract(values_all, probs_low, 0, 0)
        out_ref[:, head * HEAD_DIM : (head + 1) * HEAD_DIM] = mixed.T.astype(LOW)
        lse_ref[0, head : head + 1] = top + jnp.log(total)


def backward_kernel(heads, parts, *refs):
    qkv_refs = refs[:parts]
    grad_refs = refs[parts : 2 * parts]
    lse_refs = refs[2 * parts : 3 * parts]
    keys_segment, query_segments = refs[3 * parts : 3 * parts + 2]
    out_refs = refs[3 * parts + 2 :]
    rows = qkv_refs[0].shape[0]
    segment_col = keys_segment[0]
    for head in range(heads):
        base = head * HEAD_DIM
        keys_all = head_rows(qkv_refs, heads * HEAD_DIM + base)
        values_all = head_rows(qkv_refs, 2 * heads * HEAD_DIM + base)
        grad_keys = 0.0
        grad_values = 0.0
        for which in range(parts):
            queries = qkv_refs[which][:, base : base + HEAD_DIM]
            grad_mixed = grad_refs[which][:, base : base + HEAD_DIM]
            allowed = segment_col == query_segments[0, which : which + 1]
            logits = contract(keys_all, queries, 1, 1) * SCALING
            probs = jnp.where(allowed, jnp.exp(logits - lse_refs[which][0, head : head + 1]), 0.0)
            grad_probs = contract(values_all, grad_mixed, 1, 1)
            inner = jnp.sum(probs * grad_probs, axis=0, keepdims=True)
            grad_logits = (probs * (grad_probs - inner)).astype(LOW)
            probs_low = probs.astype(LOW)
            grad_values = grad_values + jnp.dot(
                probs_low, grad_mixed, preferred_element_type=WIDE
            )
            grad_keys = grad_keys + jnp.dot(grad_logits, queries, preferred_element_type=WIDE)
            grad_queries = contract(keys_all, grad_logits, 0, 0) * SCALING
            out_refs[which][:, base : base + HEAD_DIM] = grad_queries.T.astype(LOW)
        grad_keys = (grad_keys * SCALING).astype(LOW)
        grad_values = grad_values.astype(LOW)
        for which in range(parts):
            piece = slice(which * rows, (which + 1) * rows)
            start = heads * HEAD_DIM + base
            out_refs[which][:, start : start + HEAD_DIM] = grad_keys[piece]
            start = 2 * heads * HEAD_DIM + base
            out_refs[which][:, start : start + HEAD_DIM] = grad_values[piece]


def row_spec(rows, width):
    return pl.BlockSpec((rows, width), lambda s: (s, 0))


def cube_spec(*dims):
    return pl.BlockSpec((1,) + dims, lambda s: (s, 0, 0))


def attend_forward(which, qkv, segment_cols, segment_rows):
    parts = len(qkv)
    seqs, _, rows = segment_rows.shape
    width = qkv[0].shape[1] // 3
    heads = width // HEAD_DIM
    pairs = seqs * heads * rows * rows * parts
    return pl.pallas_call(
        functools.partial(forward_kernel, heads, parts, which),
        grid=(seqs,),
        in_specs=[row_spec(rows, 3 * width)] * parts
        + [cube_spec(parts * rows, 1), cube_spec(parts, rows)],
        out_specs=[row_spec(rows, width), cube_spec(heads, rows)],
        out_shape=[
            jax.ShapeDtypeStruct((seqs * rows, width), LOW),
            jax.ShapeDtypeStruct((seqs, heads, rows), WIDE),
        ],
        cost_estimate=pl.CostEstimate(
            flops=4 * pairs * HEAD_DIM,
            bytes_accessed=8 * seqs * rows * width * parts,
            transcendentals=pairs,
        ),
        compiler_params=pltpu.CompilerParams(vmem_limit_bytes=56 << 20),
        name="attend_forward",
    )(*qkv, segment_cols, segment_rows)


def attend_backward(qkv, grads, lses, segment_cols, segment_rows):
    parts = len(qkv)
    seqs, _, rows = segment_rows.shape
    width = qkv[0].shape[1] // 3
    heads = width // HEAD_DIM
    pairs = seqs * heads * rows * rows * parts * parts
    return pl.pallas_call(
        functools.partial(backward_kernel, heads, parts),
        grid=(seqs,),
        in_specs=[row_spec(rows, 3 * width)] * parts
        + [row_spec(rows, width)] * parts
        + [cube_spec(heads, rows)] * parts
        + [cube_spec(parts * rows, 1), cube_spec(parts, rows)],
        out_specs=[row_spec(rows, 3 * width)] * parts,
        out_shape=[jax.ShapeDtypeStruct((seqs * rows, 3 * width), LOW)] * parts,
        cost_estimate=pl.CostEstimate(
            flops=10 * pairs * HEAD_DIM,
            bytes_accessed=16 * seqs * rows * width * parts,
            transcendentals=pairs,
        ),
        compiler_params=pltpu.CompilerParams(vmem_limit_bytes=56 << 20),
        name="attend_backward",
    )(*qkv, *grads, *lses, segment_cols, segment_rows)


together = lax.optimization_barrier


def sum_everywhere(vector):
    for axis in ("dp", "mp"):
        size = lax.axis_size(axis)
        step = 1
        while step < size:
            vector = vector + lax.ppermute(vector, axis, [(k, k ^ step) for k in range(size)])
            step *= 2
    return vector


def body(
    inputs,
    segment_ids,
    cotangent,
    query_weight,
    key_weight,
    value_weight,
    out_weight,
    up_weight,
    down_weight,
    query_bias,
    value_bias,
    out_bias,
    up_bias,
    down_bias,
    first_gain,
    first_shift,
    second_gain,
    second_shift,
):
    plane, depth = lax.axis_size("dp"), lax.axis_size("mp")
    rank, level = lax.axis_index("dp"), lax.axis_index("mp")
    parts, block, width = inputs.shape
    length = block * depth
    group = depth // parts
    seqs = plane // group
    rows = group * block
    hidden = up_bias.shape[0] // plane
    heads_in_block = query_weight.shape[1] // HEAD_DIM
    sharers = plane // heads_in_block
    heads = depth // sharers
    parity = level % parts

    def route(turn, back):
        pairs = []
        for i in range(plane):
            for j in range(depth):
                e = (j + turn) % parts
                source = i * depth + j
                target = (i - i % group + j // parts) * depth + parts * (i % group) + e
                pairs.append((target, source) if back else (source, target))
        return pairs

    def pick(options, index):
        return lax.dynamic_index_in_dim(jnp.stack(options), index % parts, 0, keepdims=False)

    def enter(array):
        arrived = [
            lax.ppermute(
                lax.dynamic_index_in_dim(array, (level + turn) % parts, 0, keepdims=False),
                ("dp", "mp"),
                route(turn, False),
            )
            for turn in range(parts)
        ]
        return [pick(arrived, parity - b + parts) for b in range(parts)]

    def leave(blocks):
        arrived = [
            lax.ppermute(pick(blocks, parity - turn + parts), ("dp", "mp"), route(turn, True))
            for turn in range(parts)
        ]
        return jnp.stack([pick(arrived, e - parity + parts) for e in range(parts)])

    def gather(array):
        return lax.all_gather(array, "dp", axis=0, tiled=True)

    def gather_in_order(arrays):
        return [gather(array) for array in together(arrays)]

    def swap(array, bit):
        return lax.ppermute(array, "dp", [(k, k ^ bit) for k in range(plane)])

    def halves(array, axis, bit):
        mine = rank // bit % 2
        return [
            lax.dynamic_index_in_dim(array, index, axis, keepdims=False)
            for index in (mine, 1 - mine)
        ]

    bits = [1 << k for k in range(plane.bit_length() - 1)]

    def product_scatter(left, right):
        own, other = halves(left.reshape(plane // 2, 2, block, -1), 1, 1)

        def times(rows_of):
            return jnp.dot(
                rows_of.reshape(plane // 2 * block, -1), right, preferred_element_type=WIDE
            )

        arriving = swap(times(other).astype(LOW), 1)
        held = (times(own) + arriving.astype(WIDE)).astype(LOW)
        held = held.reshape((2,) * (len(bits) - 1) + (block, width))
        results = []
        for half, order in enumerate((bits[1:], bits[:0:-1])):
            piece = lax.slice_in_dim(
                held, half * block // 2, (half + 1) * block // 2, axis=len(bits) - 1
            )
            left_bits = bits[:0:-1]
            for bit in order:
                own, other = halves(piece, left_bits.index(bit), bit)
                left_bits = [k for k in left_bits if k != bit]
                piece = own.astype(WIDE) + swap(other, bit).astype(WIDE)
                if left_bits:
                    piece = piece.astype(LOW)
            results.append(piece)
        return jnp.concatenate(results, axis=0)

    def chain_pairs(step, up):
        if up:
            return [(k, k + 1) for k in range(step - 1, depth - 1)]
        return [(k, k - 1) for k in range(1, depth - step + 1)]

    def chain_gather(shard):
        below, above = [], []
        lower = upper = shard
        for step in range(1, depth):
            lower = lax.ppermute(lower, "mp", chain_pairs(step, True))
            upper = lax.ppermute(upper, "mp", chain_pairs(step, False))
            below.append(lower)
            above.append(upper)
        line = jnp.stack(below[::-1] + [shard] + above)
        return lax.dynamic_slice_in_dim(line, depth - 1 - level, depth, 0)

    sharing = [list(range(k, k + sharers)) for k in range(0, plane, sharers)]

    def share_out(array):
        if sharers == 1:
            return array
        return lax.all_to_all(
            array, "dp", split_axis=0, concat_axis=2, axis_index_groups=sharing, tiled=True
        )

    def share_back(array):
        if sharers == 1:
            return array
        return lax.all_to_all(
            array, "dp", split_axis=2, concat_axis=0, axis_index_groups=sharing, tiled=True
        )

    tokens = enter(inputs)
    attention_shards = jnp.stack([query_weight.T, key_weight.T, value_weight.T, out_weight])
    attention_pieces = lax.all_to_all(
        attention_shards, "dp", split_axis=1, concat_axis=2, tiled=True
    )
    attention_full = share_out(chain_gather(attention_pieces))
    attention_full = attention_full.transpose(1, 0, 2, 3).reshape(4, heads * HEAD_DIM, width)
    full_qkv = attention_full[:3].reshape(3 * heads * HEAD_DIM, width)
    full_out = attention_full[3]
    forward_shards = jnp.stack([up_weight.T, down_weight])
    forward_pieces = lax.all_to_all(forward_shards, "dp", split_axis=1, concat_axis=2, tiled=True)

    def own_heads(bias):
        table = bias.reshape(depth, heads_in_block, HEAD_DIM)
        return lax.dynamic_slice(
            table, (rank % sharers * heads, rank // sharers, 0), (heads, 1, HEAD_DIM)
        ).reshape(-1)

    qkv_bias = jnp.concatenate(
        [own_heads(query_bias), jnp.zeros((heads * HEAD_DIM,), WIDE), own_heads(value_bias)]
    )
    own_up = lax.dynamic_slice(
        up_bias.reshape(depth, plane, -1), (0, rank, 0), (depth, 1, hidden // depth)
    ).reshape(-1)

    segments = segment_ids
    for bit in bits:
        other = swap(segments, bit)
        upper = rank // bit % 2 == 1
        segments = jnp.concatenate(
            [jnp.where(upper, other, segments), jnp.where(upper, segments, other)]
        )
    segments = lax.dynamic_index_in_dim(
        segments.reshape(seqs, depth, length), level, 1, keepdims=False
    )
    segments = segments.reshape(seqs, group, parts, block).transpose(0, 2, 1, 3)
    segment_rows = segments.reshape(seqs, parts, rows)
    segment_cols = segments.reshape(seqs, parts * rows, 1)

    every = range(parts)
    gathered_inputs = [gather(tokens[b]) for b in every]
    qkv = [
        (contract(gathered_inputs[b], full_qkv, 1, 1) + qkv_bias).astype(LOW) for b in every
    ]
    full_up = lax.all_gather(forward_pieces[0], "mp", axis=0, tiled=True)
    full_down = lax.all_gather(forward_pieces[1], "mp", axis=0, tiled=True)
    cotangent, qkv = together((cotangent, qkv))
    tangents = enter(cotangent)
    attended, lses, attn_sums = [], [], []
    for b in every:
        mixed, lse = attend_forward(b, qkv, segment_cols, segment_rows)
        attended.append(mixed)
        lses.append(lse)
        attn_sums.append(product_scatter(mixed, full_out))
    first = [
        norm_forward(tokens[b].astype(WIDE) + attn_sums[b] + out_bias, first_gain, first_shift)
        for b in every
    ]
    first_low = [first[b][0].astype(LOW) for b in every]
    first_low, full_up, full_down = together((first_low, full_up, full_down))
    gathered_first = gather_in_order(first_low)
    gathered_first, tangents = together((gathered_first, tangents))
    tangents = [array.astype(WIDE) for array in tangents]
    up_proj = [contract(gathered_first[b], full_up, 1, 1) + own_up for b in every]
    hiddens = [gelu_tanh(up_proj[b]).astype(LOW) for b in every]
    ffn_sums = [product_scatter(hiddens[b], full_down) for b in every]
    second = [
        norm_forward(first[b][0] + ffn_sums[b] + down_bias, second_gain, second_shift)
        for b in every
    ]
    outputs = leave([second[b][0].astype(LOW) for b in every])

    def reduce_attention(term):
        term = term.reshape(-1, heads, HEAD_DIM, width).transpose(1, 0, 2, 3)
        return lax.psum_scatter(share_back(term), "mp", scatter_dimension=0, tiled=True)[0]

    def reduce_forward(term):
        return lax.psum_scatter(term, "mp", scatter_dimension=0, tiled=True)

    def low_sum(terms):
        return sum(terms).astype(LOW)

    def total(arrays):
        return sum(jnp.sum(array.astype(WIDE), axis=0) for array in arrays)

    grad_second_gain = total([tangents[b] * second[b][1] for b in every])
    grad_second_shift = total(tangents)
    grad_two = [
        norm_backward(tangents[b], second[b][1], second[b][2], second_gain) for b in every
    ]
    grad_ffn = [array.astype(LOW) for array in grad_two]
    grad_down_bias = total(grad_ffn)
    gathered_ffn = gather_in_order(grad_ffn)
    gathered_ffn, outputs = together((gathered_ffn, outputs))
    grad_upper = [
        jax.vjp(gelu_tanh, up_proj[b])[1](contract(gathered_ffn[b], full_down, 1, 1))[0].astype(
            LOW
        )
        for b in every
    ]
    grad_up_bias = total(grad_upper)
    back_sums = [product_scatter(grad_upper[b], full_up) for b in every]
    term_down = low_sum(contract(hiddens[b], gathered_ffn[b], 0, 0) for b in every)
    term_up = low_sum(contract(grad_upper[b], gathered_first[b], 0, 0) for b in every)
    grad_first = [grad_two[b] + back_sums[b] for b in every]
    grad_first_gain = total([grad_first[b] * first[b][1] for b in every])
    grad_first_shift = total(grad_first)
    grad_resid = [
        norm_backward(grad_first[b], first[b][1], first[b][2], first_gain) for b in every
    ]
    grad_branch = [array.astype(LOW) for array in grad_resid]
    reduced_down = reduce_forward(term_down)
    grad_branch, reduced_down = together((grad_branch, reduced_down))
    grad_out_bias = total(grad_branch)
    gathered_branch = gather_in_order(grad_branch)
    spread_up = lax.dynamic_update_slice(
        jnp.zeros((depth, plane, hidden // depth), WIDE),
        grad_up_bias.reshape(depth, 1, -1),
        (0, rank, 0),
    ).reshape(-1)
    early = (
        grad_out_bias,
        grad_down_bias,
        grad_first_gain,
        grad_first_shift,
        grad_second_gain,
        grad_second_shift,
        spread_up,
    )
    early = sum_everywhere(jnp.concatenate(early).reshape(-1, HEAD_DIM)).reshape(-1)
    gathered_branch[0], early = together((gathered_branch[0], early))
    gathered_branch, term_up = together((gathered_branch, term_up))
    reduced_up = reduce_forward(term_up)
    grad_mixed = [contract(gathered_branch[b], full_out, 1, 1).astype(LOW) for b in every]
    grad_qkv = attend_backward(qkv, grad_mixed, lses, segment_cols, segment_rows)
    input_sums = [product_scatter(grad_qkv[b], full_qkv) for b in every]
    term_out = low_sum(contract(attended[b], gathered_branch[b], 0, 0) for b in every)
    term_qkv = low_sum(contract(grad_qkv[b], gathered_inputs[b], 0, 0) for b in every)
    term_qkv, reduced_up = together((term_qkv, reduced_up))
    reduced_out = reduce_attention(term_out)
    input_sums, grad_qkv, reduced_out, reduced_down = together(
        (input_sums, grad_qkv, reduced_out, reduced_down)
    )
    grad_qkv_bias = total(grad_qkv)
    grad_inputs = leave([(grad_resid[b] + input_sums[b]).astype(LOW) for b in every]).astype(WIDE)

    def owner_exchange(term):
        return lax.all_to_all(term, "dp", split_axis=2, concat_axis=1, tiled=True)

    owned_forward = lax.all_to_all(
        jnp.stack([reduced_up, reduced_down]),
        "dp",
        split_axis=2,
        concat_axis=1,
        tiled=True,
    )
    owned_out = owner_exchange(reduced_out)
    owned_qkv = owner_exchange(reduce_attention(term_qkv))

    def spread_heads(piece):
        table = jnp.zeros((depth, heads_in_block, HEAD_DIM), WIDE)
        return lax.dynamic_update_slice(
            table,
            piece.reshape(heads, 1, HEAD_DIM),
            (rank % sharers * heads, rank // sharers, 0),
        ).reshape(-1)

    spread = heads * HEAD_DIM
    late = jnp.concatenate(
        [spread_heads(grad_qkv_bias[:spread]), spread_heads(grad_qkv_bias[2 * spread :])]
    )
    late = sum_everywhere(late.reshape(-1, HEAD_DIM)).reshape(2, width)
    narrow = early[: 6 * width].reshape(6, width)
    return (
        outputs,
        grad_inputs,
        owned_qkv[0].T.astype(WIDE),
        owned_qkv[1].T.astype(WIDE),
        owned_qkv[2].T.astype(WIDE),
        owned_out[0].astype(WIDE),
        owned_forward[0].T.astype(WIDE),
        owned_forward[1].astype(WIDE),
        late[0],
        late[1],
        narrow[0],
        early[6 * width :],
        narrow[1],
        narrow[2],
        narrow[3],
        narrow[4],
        narrow[5],
    )


def solution(mesh):
    tokens = P("dp", "mp", None)
    by_rows, by_columns, whole = P("dp", "mp"), P("mp", "dp"), P()
    in_specs = (
        (tokens, P("dp", None), tokens)
        + (by_rows,) * 3
        + (by_columns, by_rows, by_columns)
        + (whole,) * 9
    )
    out_specs = (
        (tokens, tokens) + (by_rows,) * 3 + (by_columns, by_rows, by_columns) + (whole,) * 9
    )
    return jax.shard_map(body, mesh=mesh, in_specs=in_specs, out_specs=out_specs, check_vma=False)
```

```python
import functools

import jax
import jax.numpy as jnp
from jax import lax
from jax.experimental import pallas as pl
from jax.experimental.pallas import tpu as pltpu
from jax.sharding import PartitionSpec as P

HEAD_DIM = 128
SCALING = HEAD_DIM ** (-0.5)
EPSILON = 1e-12
MASKED = -1e30
LOW = jnp.bfloat16
WIDE = jnp.float32


def contract(left, right, left_dim, right_dim):
    return lax.dot_general(
        left, right, (((left_dim,), (right_dim,)), ((), ())), preferred_element_type=WIDE
    )


def norm_forward(resid, scale_vec, shift_vec):
    average = jnp.mean(resid, axis=-1, keepdims=True)
    centered = resid - average
    variance = jnp.mean(centered * centered, axis=-1, keepdims=True)
    inv_std = lax.rsqrt(variance + EPSILON)
    normed = centered * inv_std
    return normed * scale_vec + shift_vec, normed, inv_std


def norm_backward(upstream, normed, inv_std, scale_vec):
    scaled = upstream * scale_vec
    first_mean = jnp.mean(scaled, axis=-1, keepdims=True)
    second_mean = jnp.mean(scaled * normed, axis=-1, keepdims=True)
    return inv_std * (scaled - first_mean - normed * second_mean)


def gelu_tanh(values_in):
    return jax.nn.gelu(values_in, approximate=True)


def head_rows(refs, column):
    return jnp.concatenate([ref[:, column : column + HEAD_DIM] for ref in refs], axis=0)


def forward_kernel(heads, parts, which, *refs):
    qkv_refs = refs[:parts]
    keys_segment, query_segments, out_ref, lse_ref = refs[parts:]
    segment_col = keys_segment[0]
    segment_row = query_segments[0, which : which + 1]
    allowed = segment_col == segment_row
    for head in range(heads):
        queries = qkv_refs[which][:, head * HEAD_DIM : (head + 1) * HEAD_DIM]
        keys_all = head_rows(qkv_refs, (heads + head) * HEAD_DIM)
        values_all = head_rows(qkv_refs, (2 * heads + head) * HEAD_DIM)
        logits = jnp.where(allowed, contract(keys_all, queries, 1, 1) * SCALING, MASKED)
        top = jnp.max(logits, axis=0, keepdims=True)
        expo = jnp.exp(logits - top)
        total = jnp.sum(expo, axis=0, keepdims=True)
        probs_low = (expo * (1.0 / total)).astype(LOW)
        mixed = contract(values_all, probs_low, 0, 0)
        out_ref[:, head * HEAD_DIM : (head + 1) * HEAD_DIM] = mixed.T.astype(LOW)
        lse_ref[0, head : head + 1] = top + jnp.log(total)


def backward_kernel(heads, parts, *refs):
    qkv_refs = refs[:parts]
    grad_refs = refs[parts : 2 * parts]
    lse_refs = refs[2 * parts : 3 * parts]
    keys_segment, query_segments = refs[3 * parts : 3 * parts + 2]
    out_refs = refs[3 * parts + 2 : 4 * parts + 2]
    bias_ref = refs[4 * parts + 2]
    rows = qkv_refs[0].shape[0]
    segment_col = keys_segment[0]
    bias_ref[...] = jnp.zeros_like(bias_ref)
    for head in range(heads):
        base = head * HEAD_DIM
        keys_all = head_rows(qkv_refs, heads * HEAD_DIM + base)
        values_all = head_rows(qkv_refs, 2 * heads * HEAD_DIM + base)
        grad_keys = 0.0
        grad_values = 0.0
        query_bias = 0.0
        for which in range(parts):
            queries = qkv_refs[which][:, base : base + HEAD_DIM]
            grad_mixed = grad_refs[which][:, base : base + HEAD_DIM]
            allowed = segment_col == query_segments[0, which : which + 1]
            logits = contract(keys_all, queries, 1, 1) * SCALING
            probs = jnp.where(allowed, jnp.exp(logits - lse_refs[which][0, head : head + 1]), 0.0)
            grad_probs = contract(values_all, grad_mixed, 1, 1)
            inner = jnp.sum(probs * grad_probs, axis=0, keepdims=True)
            grad_logits = (probs * (grad_probs - inner)).astype(LOW)
            probs_low = probs.astype(LOW)
            grad_values = grad_values + jnp.dot(
                probs_low, grad_mixed, preferred_element_type=WIDE
            )
            grad_keys = grad_keys + jnp.dot(grad_logits, queries, preferred_element_type=WIDE)
            grad_queries = (contract(keys_all, grad_logits, 0, 0) * SCALING).T.astype(LOW)
            query_bias = query_bias + jnp.sum(grad_queries.astype(WIDE), axis=0, keepdims=True)
            out_refs[which][:, base : base + HEAD_DIM] = grad_queries
        grad_keys = (grad_keys * SCALING).astype(LOW)
        grad_values = grad_values.astype(LOW)
        bias_ref[0, :, base : base + HEAD_DIM] = query_bias
        start = 2 * heads * HEAD_DIM + base
        bias_ref[0, :, start : start + HEAD_DIM] = jnp.sum(
            grad_values.astype(WIDE), axis=0, keepdims=True
        )
        for which in range(parts):
            piece = slice(which * rows, (which + 1) * rows)
            start = heads * HEAD_DIM + base
            out_refs[which][:, start : start + HEAD_DIM] = grad_keys[piece]
            start = 2 * heads * HEAD_DIM + base
            out_refs[which][:, start : start + HEAD_DIM] = grad_values[piece]


def row_spec(rows, width):
    return pl.BlockSpec((rows, width), lambda s: (s, 0))


def cube_spec(*dims):
    return pl.BlockSpec((1,) + dims, lambda s: (s, 0, 0))


def attend_forward(which, qkv, segment_cols, segment_rows):
    parts = len(qkv)
    seqs, _, rows = segment_rows.shape
    width = qkv[0].shape[1] // 3
    heads = width // HEAD_DIM
    pairs = seqs * heads * rows * rows * parts
    return pl.pallas_call(
        functools.partial(forward_kernel, heads, parts, which),
        grid=(seqs,),
        in_specs=[row_spec(rows, 3 * width)] * parts
        + [cube_spec(parts * rows, 1), cube_spec(parts, rows)],
        out_specs=[row_spec(rows, width), cube_spec(heads, rows)],
        out_shape=[
            jax.ShapeDtypeStruct((seqs * rows, width), LOW),
            jax.ShapeDtypeStruct((seqs, heads, rows), WIDE),
        ],
        cost_estimate=pl.CostEstimate(
            flops=4 * pairs * HEAD_DIM,
            bytes_accessed=8 * seqs * rows * width * parts,
            transcendentals=pairs,
        ),
        compiler_params=pltpu.CompilerParams(vmem_limit_bytes=56 << 20),
        name="attend_forward",
    )(*qkv, segment_cols, segment_rows)


def attend_backward(qkv, grads, lses, segment_cols, segment_rows):
    parts = len(qkv)
    seqs, _, rows = segment_rows.shape
    width = qkv[0].shape[1] // 3
    heads = width // HEAD_DIM
    pairs = seqs * heads * rows * rows * parts * parts
    results = pl.pallas_call(
        functools.partial(backward_kernel, heads, parts),
        grid=(seqs,),
        in_specs=[row_spec(rows, 3 * width)] * parts
        + [row_spec(rows, width)] * parts
        + [cube_spec(heads, rows)] * parts
        + [cube_spec(parts * rows, 1), cube_spec(parts, rows)],
        out_specs=[row_spec(rows, 3 * width)] * parts + [cube_spec(1, 3 * width)],
        out_shape=[jax.ShapeDtypeStruct((seqs * rows, 3 * width), LOW)] * parts
        + [jax.ShapeDtypeStruct((seqs, 1, 3 * width), WIDE)],
        cost_estimate=pl.CostEstimate(
            flops=10 * pairs * HEAD_DIM,
            bytes_accessed=16 * seqs * rows * width * parts,
            transcendentals=pairs,
        ),
        compiler_params=pltpu.CompilerParams(vmem_limit_bytes=56 << 20),
        name="attend_backward",
    )(*qkv, *grads, *lses, segment_cols, segment_rows)
    return list(results[:parts]), jnp.sum(results[parts], axis=(0, 1))


together = lax.optimization_barrier


def scatter_plan(bits, parts):
    plan = []
    for part in range(parts):
        order = bits if part % 2 == 0 else bits[::-1]
        held = patterns_of(bits)
        for bit in order:
            plan.append((part, bit, tuple(p for p in held if p & bit)))
            held = [p for p in held if not p & bit]
    return plan


def patterns_of(bits):
    patterns = [0]
    for bit in bits:
        patterns += [p | bit for p in patterns]
    return patterns


def scatter_kernel(bits, parts, *refs):
    left_refs = refs[:parts]
    right_ref, out_ref, far, arrived, held, passed = refs[parts : parts + 6]
    core_send, core_recv, ring_send, ring_recv = refs[parts + 6 :]
    rank = lax.axis_index("dp")
    block, width = out_ref.shape[1:]
    stride = min(512, width)

    def across(bit):
        return rank + bit - 2 * bit * (rank // bit % 2)

    barrier = pltpu.get_barrier_semaphore()
    partners = [1] + list(bits)
    for bit in partners:
        pl.semaphore_signal(
            barrier,
            inc=1,
            device_id={"dp": across(bit)},
            device_id_type=pl.DeviceIdType.MESH,
        )
    pl.semaphore_wait(barrier, len(partners))

    patterns = patterns_of(bits)
    place = {p: k for k, p in enumerate(patterns)}

    def tile_rows(part, pattern):
        owner = rank
        for bit in partners:
            if pattern & bit:
                owner = owner + bit - 2 * bit * (rank // bit % 2)
        return left_refs[part].at[pl.ds(pl.multiple_of(owner * block, block), block)]

    def by_columns(function):
        @pl.loop(0, width // stride)
        def _(step):
            function(pl.ds(pl.multiple_of(step * stride, stride), stride))

    core_copies = {}
    ring_copies = {}
    slot = 0
    plan = scatter_plan(bits, parts)
    for part, bit, moved in plan:
        for pattern in moved:
            ring_copies[part, bit, pattern] = (
                slot,
                pltpu.make_async_remote_copy(
                    src_ref=held.at[part, place[pattern]],
                    dst_ref=passed.at[slot],
                    send_sem=ring_send.at[slot],
                    recv_sem=ring_recv.at[slot],
                    device_id={"dp": across(bit)},
                    device_id_type=pl.DeviceIdType.MESH,
                ),
            )
            slot += 1

    def far_tile(part, pattern):
        rows = tile_rows(part, pattern | 1)
        index = part * len(patterns) + place[pattern]

        def columns(window):
            far[index, :, window] = jnp.dot(
                rows[...], right_ref[:, window], preferred_element_type=WIDE
            ).astype(LOW)

        by_columns(columns)
        copy = pltpu.make_async_remote_copy(
            src_ref=far.at[index],
            dst_ref=arrived.at[index],
            send_sem=core_send.at[index],
            recv_sem=core_recv.at[index],
            device_id={"dp": across(1)},
            device_id_type=pl.DeviceIdType.MESH,
        )
        copy.start()
        core_copies[part, pattern] = (index, copy)

    def near_tile(part, pattern):
        rows = tile_rows(part, pattern)
        index, copy = core_copies[part, pattern]
        copy.wait_recv()

        def columns(window):
            value = jnp.dot(
                rows[...], right_ref[:, window], preferred_element_type=WIDE
            ) + arrived[index, :, window].astype(WIDE)
            if pattern:
                held[part, place[pattern], :, window] = value.astype(LOW)
            else:
                out_ref[part, :, window] = value

        by_columns(columns)

    def send(part, bit, moved):
        for pattern in moved:
            ring_copies[part, bit, pattern][1].start()

    def take(part, bit, moved):
        for pattern in moved:
            number, copy = ring_copies[part, bit, pattern]
            copy.wait_recv()
            target = pattern - bit

            def columns(window):
                coming = passed[number, :, window].astype(WIDE)
                if target:
                    old = held[part, place[target], :, window].astype(WIDE)
                    held[part, place[target], :, window] = (old + coming).astype(LOW)
                else:
                    out_ref[part, :, window] = out_ref[part, :, window] + coming

            by_columns(columns)

    steps = [[entry for entry in plan if entry[0] == part] for part in range(parts)]
    first = [steps[part][0] for part in range(parts)]
    urgent = [
        (part, pattern)
        for tiles in zip(*[sorted(entry[2], reverse=True) for entry in first])
        for part, pattern in enumerate(tiles)
    ]
    others = [
        (part, pattern)
        for pattern in sorted(patterns, reverse=True)
        for part in range(parts)
        if (part, pattern) not in urgent
    ]
    queue = urgent + others
    ahead = 2 * parts
    for entry in queue[:ahead]:
        far_tile(*entry)
    for number, (part, pattern) in enumerate(queue):
        near_tile(part, pattern)
        if (part, pattern) in urgent:
            ring_copies[part, first[part][1], pattern][1].start()
        if number + ahead < len(queue):
            far_tile(*queue[number + ahead])
    for level in range(len(bits)):
        for part in range(parts):
            take(*steps[part][level])
            if level + 1 < len(bits):
                send(*steps[part][level + 1])
    for _, copy in list(core_copies.values()) + list(ring_copies.values()):
        copy.wait_send()


def product_scatter(lefts, right, collective_id):
    parts = len(lefts)
    plane = lax.axis_size("dp")
    bits = [1 << k for k in range(1, plane.bit_length() - 1)]
    rows, depth = lefts[0].shape
    width = right.shape[1]
    block = rows // plane
    tiles = plane // 2
    passes = sum(len(moved) for _, _, moved in scatter_plan(bits, parts))
    sent = parts * tiles * block * width * 2 * 2
    result = pl.pallas_call(
        functools.partial(scatter_kernel, bits, parts),
        out_shape=jax.ShapeDtypeStruct((parts, block, width), WIDE),
        in_specs=[pl.BlockSpec(memory_space=pltpu.VMEM)] * (parts + 1),
        out_specs=pl.BlockSpec(memory_space=pltpu.VMEM),
        scratch_shapes=[
            pltpu.VMEM((parts * tiles, block, width), LOW),
            pltpu.VMEM((parts * tiles, block, width), LOW),
            pltpu.VMEM((parts, tiles, block, width), LOW),
            pltpu.VMEM((passes, block, width), LOW),
            pltpu.SemaphoreType.DMA((parts * tiles,)),
            pltpu.SemaphoreType.DMA((parts * tiles,)),
            pltpu.SemaphoreType.DMA((passes,)),
            pltpu.SemaphoreType.DMA((passes,)),
        ],
        cost_estimate=pl.CostEstimate(
            flops=2 * parts * rows * depth * width,
            bytes_accessed=8 * sent,
            transcendentals=0,
        ),
        compiler_params=pltpu.CompilerParams(
            collective_id=collective_id, has_side_effects=True, vmem_limit_bytes=60 << 20
        ),
        name="product_scatter",
    )(*lefts, right)
    return [result[b] for b in range(parts)]


def sum_everywhere(vector):
    for axis in ("dp", "mp"):
        size = lax.axis_size(axis)
        step = 1
        while step < size:
            vector = vector + lax.ppermute(vector, axis, [(k, k ^ step) for k in range(size)])
            step *= 2
    return vector


def body(
    inputs,
    segment_ids,
    cotangent,
    query_weight,
    key_weight,
    value_weight,
    out_weight,
    up_weight,
    down_weight,
    query_bias,
    value_bias,
    out_bias,
    up_bias,
    down_bias,
    first_gain,
    first_shift,
    second_gain,
    second_shift,
):
    plane, depth = lax.axis_size("dp"), lax.axis_size("mp")
    rank, level = lax.axis_index("dp"), lax.axis_index("mp")
    parts, block, width = inputs.shape
    length = block * depth
    group = depth // parts
    seqs = plane // group
    rows = group * block
    hidden = up_bias.shape[0] // plane
    heads_in_block = query_weight.shape[1] // HEAD_DIM
    sharers = plane // heads_in_block
    heads = depth // sharers
    parity = level % parts

    def route(turn, back):
        pairs = []
        for i in range(plane):
            for j in range(depth):
                e = (j + turn) % parts
                source = i * depth + j
                target = (i - i % group + j // parts) * depth + parts * (i % group) + e
                pairs.append((target, source) if back else (source, target))
        return pairs

    def pick(options, index):
        return lax.dynamic_index_in_dim(jnp.stack(options), index % parts, 0, keepdims=False)

    def enter(array):
        arrived = [
            lax.ppermute(
                lax.dynamic_index_in_dim(array, (level + turn) % parts, 0, keepdims=False),
                ("dp", "mp"),
                route(turn, False),
            )
            for turn in range(parts)
        ]
        return [pick(arrived, parity - b + parts) for b in range(parts)]

    def leave_picks(blocks):
        return [pick(blocks, parity - turn + parts) for turn in range(parts)]

    def leave_sent(picks):
        return [
            lax.ppermute(picks[turn], ("dp", "mp"), route(turn, True)) for turn in range(parts)
        ]

    def leave_placed(arrived):
        return jnp.stack([pick(arrived, e - parity + parts) for e in range(parts)])

    def gather(array):
        return lax.all_gather(array, "dp", axis=0, tiled=True)

    def gather_in_order(arrays):
        return [gather(array) for array in together(arrays)]

    def swap(array, bit):
        return lax.ppermute(array, "dp", [(k, k ^ bit) for k in range(plane)])

    bits = [1 << k for k in range(plane.bit_length() - 1)]

    def chain_pairs(step, up):
        if up:
            return [(k, k + 1) for k in range(step - 1, depth - 1)]
        return [(k, k - 1) for k in range(1, depth - step + 1)]

    def chain_gather(shard):
        below, above = [], []
        lower = upper = shard
        for step in range(1, depth):
            lower = lax.ppermute(lower, "mp", chain_pairs(step, True))
            upper = lax.ppermute(upper, "mp", chain_pairs(step, False))
            below.append(lower)
            above.append(upper)
        line = jnp.stack(below[::-1] + [shard] + above)
        return lax.dynamic_slice_in_dim(line, depth - 1 - level, depth, 0)

    sharing = [list(range(k, k + sharers)) for k in range(0, plane, sharers)]

    def share_out(array):
        if sharers == 1:
            return array
        return lax.all_to_all(
            array, "dp", split_axis=0, concat_axis=2, axis_index_groups=sharing, tiled=True
        )

    def share_back(array):
        if sharers == 1:
            return array
        return lax.all_to_all(
            array, "dp", split_axis=2, concat_axis=0, axis_index_groups=sharing, tiled=True
        )

    tokens = enter(inputs)
    attention_shards = jnp.stack([query_weight.T, key_weight.T, value_weight.T, out_weight])
    attention_shards = attention_shards.reshape(4, plane, -1, width // plane)
    attention_pieces = lax.all_to_all(
        attention_shards.transpose(1, 0, 2, 3).reshape(-1, width // plane),
        "dp",
        split_axis=0,
        concat_axis=1,
        tiled=True,
    ).reshape(4, -1, width)
    tokens, attention_pieces = together((tokens, attention_pieces))
    attention_full = share_out(chain_gather(attention_pieces))
    attention_full = attention_full.transpose(1, 0, 2, 3).reshape(4, heads * HEAD_DIM, width)
    full_qkv = attention_full[:3].reshape(3 * heads * HEAD_DIM, width)
    full_out = attention_full[3]
    up_piece, down_piece = [
        lax.all_to_all(shard, "dp", split_axis=0, concat_axis=1, tiled=True)
        for shard in (up_weight.T, down_weight)
    ]

    def own_heads(bias):
        table = bias.reshape(depth, heads_in_block, HEAD_DIM)
        return lax.dynamic_slice(
            table, (rank % sharers * heads, rank // sharers, 0), (heads, 1, HEAD_DIM)
        ).reshape(-1)

    qkv_bias = jnp.concatenate(
        [own_heads(query_bias), jnp.zeros((heads * HEAD_DIM,), WIDE), own_heads(value_bias)]
    )
    own_up = lax.dynamic_slice(
        up_bias.reshape(depth, plane, -1), (0, rank, 0), (depth, 1, hidden // depth)
    ).reshape(-1)

    segments = segment_ids
    for bit in bits:
        other = swap(segments, bit)
        upper = rank // bit % 2 == 1
        segments = jnp.concatenate(
            [jnp.where(upper, other, segments), jnp.where(upper, segments, other)]
        )
    segments = lax.dynamic_index_in_dim(
        segments.reshape(seqs, depth, length), level, 1, keepdims=False
    )
    segments = segments.reshape(seqs, group, parts, block).transpose(0, 2, 1, 3)
    segment_rows = segments.reshape(seqs, parts, rows)
    segment_cols = segments.reshape(seqs, parts * rows, 1)

    every = range(parts)
    gathered_inputs = [gather(tokens[b]) for b in every]
    qkv = [
        (contract(gathered_inputs[b], full_qkv, 1, 1) + qkv_bias).astype(LOW) for b in every
    ]
    full_up = lax.all_gather(up_piece, "mp", axis=0, tiled=True)
    full_down = lax.all_gather(down_piece, "mp", axis=0, tiled=True)
    cotangent, qkv = together((cotangent, qkv))
    tangents = enter(cotangent)
    attended, lses = [], []
    for b in every:
        mixed, lse = attend_forward(b, qkv, segment_cols, segment_rows)
        attended.append(mixed)
        lses.append(lse)
    attn_sums = product_scatter(attended, full_out, 1)
    first = [
        norm_forward(tokens[b].astype(WIDE) + attn_sums[b] + out_bias, first_gain, first_shift)
        for b in every
    ]
    first_low = [first[b][0].astype(LOW) for b in every]
    first_low, full_up, full_down = together((first_low, full_up, full_down))
    gathered_first = gather_in_order(first_low)
    gathered_first[-1], tangents = together((gathered_first[-1], tangents))
    tangents = [array.astype(WIDE) for array in tangents]
    up_proj = [contract(gathered_first[b], full_up, 1, 1) + own_up for b in every]
    hiddens = [gelu_tanh(up_proj[b]).astype(LOW) for b in every]
    ffn_sums = product_scatter(hiddens, full_down, 2)
    second = [
        norm_forward(first[b][0] + ffn_sums[b] + down_bias, second_gain, second_shift)
        for b in every
    ]
    outputs = leave_placed(
        leave_sent(leave_picks([second[b][0].astype(LOW) for b in every]))
    )

    def share_attention(term):
        return share_back(term.reshape(-1, heads, HEAD_DIM, width).transpose(1, 0, 2, 3))

    def reduce_attention(term):
        return lax.psum_scatter(share_attention(term), "mp", scatter_dimension=0, tiled=True)[0]

    def reduce_forward(term):
        return lax.psum_scatter(term, "mp", scatter_dimension=0, tiled=True)

    def owner_exchange(term):
        return lax.all_to_all(
            term.reshape(-1, width), "dp", split_axis=1, concat_axis=0, tiled=True
        )

    def low_sum(terms):
        return sum(terms).astype(LOW)

    def total(arrays):
        return sum(jnp.sum(array.astype(WIDE), axis=0) for array in arrays)

    grad_second_gain = total([tangents[b] * second[b][1] for b in every])
    grad_second_shift = total(tangents)
    grad_two = [
        norm_backward(tangents[b], second[b][1], second[b][2], second_gain) for b in every
    ]
    grad_ffn = [array.astype(LOW) for array in grad_two]
    grad_down_bias = total(grad_ffn)
    gathered_ffn = gather_in_order(grad_ffn)
    gathered_ffn[-1], outputs = together((gathered_ffn[-1], outputs))
    grad_upper = [
        jax.vjp(gelu_tanh, up_proj[b])[1](contract(gathered_ffn[b], full_down, 1, 1))[0].astype(
            LOW
        )
        for b in every
    ]
    grad_up_bias = total(grad_upper)
    back_sums = product_scatter(grad_upper, full_up, 2)
    term_down = low_sum(contract(hiddens[b], gathered_ffn[b], 0, 0) for b in every)
    term_up = low_sum(contract(grad_upper[b], gathered_first[b], 0, 0) for b in every)
    grad_first = [grad_two[b] + back_sums[b] for b in every]
    grad_first_gain = total([grad_first[b] * first[b][1] for b in every])
    grad_first_shift = total(grad_first)
    grad_resid = [
        norm_backward(grad_first[b], first[b][1], first[b][2], first_gain) for b in every
    ]
    grad_branch = [array.astype(LOW) for array in grad_resid]
    reduced_down = reduce_forward(term_down)
    grad_branch, reduced_down = together((grad_branch, reduced_down))
    grad_out_bias = total(grad_branch)
    gathered_branch = gather_in_order(grad_branch)
    spread_up = lax.dynamic_update_slice(
        jnp.zeros((depth, plane, hidden // depth), WIDE),
        grad_up_bias.reshape(depth, 1, -1),
        (0, rank, 0),
    ).reshape(-1)
    early = (
        grad_out_bias,
        grad_down_bias,
        grad_first_gain,
        grad_first_shift,
        grad_second_gain,
        grad_second_shift,
        spread_up,
    )
    early = sum_everywhere(jnp.concatenate(early).reshape(-1, HEAD_DIM)).reshape(-1)
    owned_down = owner_exchange(reduced_down)
    gathered_branch[-1], early, owned_down = together((gathered_branch[-1], early, owned_down))
    gathered_branch[-1], term_up = together((gathered_branch[-1], term_up))
    reduced_up = reduce_forward(term_up)
    grad_mixed = [contract(gathered_branch[b], full_out, 1, 1).astype(LOW) for b in every]
    grad_qkv, grad_qkv_bias = attend_backward(qkv, grad_mixed, lses, segment_cols, segment_rows)

    def spread_heads(piece):
        table = jnp.zeros((depth, heads_in_block, HEAD_DIM), WIDE)
        return lax.dynamic_update_slice(
            table,
            piece.reshape(heads, 1, HEAD_DIM),
            (rank % sharers * heads, rank // sharers, 0),
        ).reshape(-1)

    spread = heads * HEAD_DIM
    late = jnp.concatenate(
        [spread_heads(grad_qkv_bias[:spread]), spread_heads(grad_qkv_bias[2 * spread :])]
    )
    late = sum_everywhere(late.reshape(-1, HEAD_DIM)).reshape(2, width)
    reduced_out = reduce_attention(
        low_sum(contract(attended[b], gathered_branch[b], 0, 0) for b in every)
    )
    term_qkv = low_sum(contract(grad_qkv[b], gathered_inputs[b], 0, 0) for b in every)
    term_qkv, reduced_up = together((term_qkv, reduced_up))
    shared_qkv = share_attention(term_qkv)
    owned_up = owner_exchange(reduced_up)
    grad_qkv, shared_qkv, late, owned_up = together((grad_qkv, shared_qkv, late, owned_up))
    input_sums = product_scatter(grad_qkv, full_qkv, 3)
    reduced_qkv = lax.psum_scatter(shared_qkv, "mp", scatter_dimension=0, tiled=True)[0]
    grad_low = [(grad_resid[b] + input_sums[b]).astype(LOW) for b in every]
    leaving = leave_sent(leave_picks(grad_low))
    leaving[0], reduced_out, reduced_qkv = together((leaving[0], reduced_out, reduced_qkv))
    grad_inputs = leave_placed(leaving).astype(WIDE)

    owned_out = owner_exchange(reduced_out)
    owned_qkv = owner_exchange(reduced_qkv)
    owned_qkv = owned_qkv.reshape(plane, 3, -1, width // plane).transpose(1, 0, 2, 3)
    owned_qkv = owned_qkv.reshape(3, -1, width // plane)

    narrow = early[: 6 * width].reshape(6, width)
    return (
        outputs,
        grad_inputs,
        owned_qkv[0].T.astype(WIDE),
        owned_qkv[1].T.astype(WIDE),
        owned_qkv[2].T.astype(WIDE),
        owned_out.astype(WIDE),
        owned_up.T.astype(WIDE),
        owned_down.astype(WIDE),
        late[0],
        late[1],
        narrow[0],
        early[6 * width :],
        narrow[1],
        narrow[2],
        narrow[3],
        narrow[4],
        narrow[5],
    )


def solution(mesh):
    tokens = P("dp", "mp", None)
    by_rows, by_columns, whole = P("dp", "mp"), P("mp", "dp"), P()
    in_specs = (
        (tokens, P("dp", None), tokens)
        + (by_rows,) * 3
        + (by_columns, by_rows, by_columns)
        + (whole,) * 9
    )
    out_specs = (
        (tokens, tokens) + (by_rows,) * 3 + (by_columns, by_rows, by_columns) + (whole,) * 9
    )
    return jax.shard_map(body, mesh=mesh, in_specs=in_specs, out_specs=out_specs, check_vma=False)
```

```python
import functools

import jax
import jax.numpy as jnp
from jax import lax
from jax.experimental import pallas as pl
from jax.experimental.pallas import tpu as pltpu
from jax.sharding import PartitionSpec as P

HEAD_DIM = 128
SCALING = HEAD_DIM ** (-0.5)
EPSILON = 1e-12
MASKED = -1e30
LOW = jnp.bfloat16
WIDE = jnp.float32


def contract(left, right, left_dim, right_dim):
    return lax.dot_general(
        left, right, (((left_dim,), (right_dim,)), ((), ())), preferred_element_type=WIDE
    )


def norm_forward(resid, scale_vec, shift_vec):
    average = jnp.mean(resid, axis=-1, keepdims=True)
    centered = resid - average
    variance = jnp.mean(centered * centered, axis=-1, keepdims=True)
    inv_std = lax.rsqrt(variance + EPSILON)
    normed = centered * inv_std
    return normed * scale_vec + shift_vec, normed, inv_std


def norm_backward(upstream, normed, inv_std, scale_vec):
    scaled = upstream * scale_vec
    first_mean = jnp.mean(scaled, axis=-1, keepdims=True)
    second_mean = jnp.mean(scaled * normed, axis=-1, keepdims=True)
    return inv_std * (scaled - first_mean - normed * second_mean)


def gelu_tanh(values_in):
    return jax.nn.gelu(values_in, approximate=True)


def head_rows(refs, column):
    return jnp.concatenate([ref[:, column : column + HEAD_DIM] for ref in refs], axis=0)


def forward_kernel(heads, parts, which, *refs):
    qkv_refs = refs[:parts]
    keys_segment, query_segments, out_ref, lse_ref = refs[parts:]
    segment_col = keys_segment[0]
    segment_row = query_segments[0, which : which + 1]
    allowed = segment_col == segment_row
    for head in range(heads):
        queries = qkv_refs[which][:, head * HEAD_DIM : (head + 1) * HEAD_DIM]
        keys_all = head_rows(qkv_refs, (heads + head) * HEAD_DIM)
        values_all = head_rows(qkv_refs, (2 * heads + head) * HEAD_DIM)
        logits = jnp.where(allowed, contract(keys_all, queries, 1, 1) * SCALING, MASKED)
        top = jnp.max(logits, axis=0, keepdims=True)
        expo = jnp.exp(logits - top)
        total = jnp.sum(expo, axis=0, keepdims=True)
        probs_low = (expo * (1.0 / total)).astype(LOW)
        mixed = contract(values_all, probs_low, 0, 0)
        out_ref[:, head * HEAD_DIM : (head + 1) * HEAD_DIM] = mixed.T.astype(LOW)
        lse_ref[0, head : head + 1] = top + jnp.log(total)


def backward_kernel(heads, parts, *refs):
    qkv_refs = refs[:parts]
    grad_refs = refs[parts : 2 * parts]
    lse_refs = refs[2 * parts : 3 * parts]
    keys_segment, query_segments = refs[3 * parts : 3 * parts + 2]
    out_refs = refs[3 * parts + 2 : 4 * parts + 2]
    bias_ref = refs[4 * parts + 2]
    rows = qkv_refs[0].shape[0]
    segment_col = keys_segment[0]
    bias_ref[...] = jnp.zeros_like(bias_ref)
    for head in range(heads):
        base = head * HEAD_DIM
        keys_all = head_rows(qkv_refs, heads * HEAD_DIM + base)
        values_all = head_rows(qkv_refs, 2 * heads * HEAD_DIM + base)
        grad_keys = 0.0
        grad_values = 0.0
        query_bias = 0.0
        for which in range(parts):
            queries = qkv_refs[which][:, base : base + HEAD_DIM]
            grad_mixed = grad_refs[which][:, base : base + HEAD_DIM]
            allowed = segment_col == query_segments[0, which : which + 1]
            logits = contract(keys_all, queries, 1, 1) * SCALING
            probs = jnp.where(allowed, jnp.exp(logits - lse_refs[which][0, head : head + 1]), 0.0)
            grad_probs = contract(values_all, grad_mixed, 1, 1)
            inner = jnp.sum(probs * grad_probs, axis=0, keepdims=True)
            grad_logits = (probs * (grad_probs - inner)).astype(LOW)
            probs_low = probs.astype(LOW)
            grad_values = grad_values + jnp.dot(
                probs_low, grad_mixed, preferred_element_type=WIDE
            )
            grad_keys = grad_keys + jnp.dot(grad_logits, queries, preferred_element_type=WIDE)
            grad_queries = (contract(keys_all, grad_logits, 0, 0) * SCALING).T.astype(LOW)
            query_bias = query_bias + jnp.sum(grad_queries.astype(WIDE), axis=0, keepdims=True)
            out_refs[which][:, base : base + HEAD_DIM] = grad_queries
        grad_keys = (grad_keys * SCALING).astype(LOW)
        grad_values = grad_values.astype(LOW)
        bias_ref[0, :, base : base + HEAD_DIM] = query_bias
        start = 2 * heads * HEAD_DIM + base
        bias_ref[0, :, start : start + HEAD_DIM] = jnp.sum(
            grad_values.astype(WIDE), axis=0, keepdims=True
        )
        for which in range(parts):
            piece = slice(which * rows, (which + 1) * rows)
            start = heads * HEAD_DIM + base
            out_refs[which][:, start : start + HEAD_DIM] = grad_keys[piece]
            start = 2 * heads * HEAD_DIM + base
            out_refs[which][:, start : start + HEAD_DIM] = grad_values[piece]


def row_spec(rows, width):
    return pl.BlockSpec((rows, width), lambda s: (s, 0))


def cube_spec(*dims):
    return pl.BlockSpec((1,) + dims, lambda s: (s, 0, 0))


def attend_forward(which, qkv, segment_cols, segment_rows):
    parts = len(qkv)
    seqs, _, rows = segment_rows.shape
    width = qkv[0].shape[1] // 3
    heads = width // HEAD_DIM
    pairs = seqs * heads * rows * rows * parts
    return pl.pallas_call(
        functools.partial(forward_kernel, heads, parts, which),
        grid=(seqs,),
        in_specs=[row_spec(rows, 3 * width)] * parts
        + [cube_spec(parts * rows, 1), cube_spec(parts, rows)],
        out_specs=[row_spec(rows, width), cube_spec(heads, rows)],
        out_shape=[
            jax.ShapeDtypeStruct((seqs * rows, width), LOW),
            jax.ShapeDtypeStruct((seqs, heads, rows), WIDE),
        ],
        cost_estimate=pl.CostEstimate(
            flops=4 * pairs * HEAD_DIM,
            bytes_accessed=8 * seqs * rows * width * parts,
            transcendentals=pairs,
        ),
        compiler_params=pltpu.CompilerParams(vmem_limit_bytes=56 << 20),
        name="attend_forward",
    )(*qkv, segment_cols, segment_rows)


def attend_backward(qkv, grads, lses, segment_cols, segment_rows):
    parts = len(qkv)
    seqs, _, rows = segment_rows.shape
    width = qkv[0].shape[1] // 3
    heads = width // HEAD_DIM
    pairs = seqs * heads * rows * rows * parts * parts
    results = pl.pallas_call(
        functools.partial(backward_kernel, heads, parts),
        grid=(seqs,),
        in_specs=[row_spec(rows, 3 * width)] * parts
        + [row_spec(rows, width)] * parts
        + [cube_spec(heads, rows)] * parts
        + [cube_spec(parts * rows, 1), cube_spec(parts, rows)],
        out_specs=[row_spec(rows, 3 * width)] * parts + [cube_spec(1, 3 * width)],
        out_shape=[jax.ShapeDtypeStruct((seqs * rows, 3 * width), LOW)] * parts
        + [jax.ShapeDtypeStruct((seqs, 1, 3 * width), WIDE)],
        cost_estimate=pl.CostEstimate(
            flops=10 * pairs * HEAD_DIM,
            bytes_accessed=16 * seqs * rows * width * parts,
            transcendentals=pairs,
        ),
        compiler_params=pltpu.CompilerParams(vmem_limit_bytes=56 << 20),
        name="attend_backward",
    )(*qkv, *grads, *lses, segment_cols, segment_rows)
    return list(results[:parts]), jnp.sum(results[parts], axis=(0, 1))


together = lax.optimization_barrier


def scatter_plan(bits, parts):
    plan = []
    for part in range(parts):
        order = bits if part % 2 == 0 else bits[::-1]
        held = patterns_of(bits)
        for bit in order:
            plan.append((part, bit, tuple(p for p in held if p & bit)))
            held = [p for p in held if not p & bit]
    return plan


def patterns_of(bits):
    patterns = [0]
    for bit in bits:
        patterns += [p | bit for p in patterns]
    return patterns


def scatter_kernel(bits, parts, *refs):
    left_refs = refs[:parts]
    right_ref, out_ref, far, arrived, held, passed = refs[parts : parts + 6]
    core_send, core_recv, ring_send, ring_recv = refs[parts + 6 :]
    rank = lax.axis_index("dp")
    block, width = out_ref.shape[1:]
    stride = min(512, width)

    def across(bit):
        return rank + bit - 2 * bit * (rank // bit % 2)

    barrier = pltpu.get_barrier_semaphore()
    partners = [1] + list(bits)
    for bit in partners:
        pl.semaphore_signal(
            barrier,
            inc=1,
            device_id={"dp": across(bit)},
            device_id_type=pl.DeviceIdType.MESH,
        )
    pl.semaphore_wait(barrier, len(partners))

    patterns = patterns_of(bits)
    place = {p: k for k, p in enumerate(patterns)}

    def tile_rows(part, pattern):
        owner = rank
        for bit in partners:
            if pattern & bit:
                owner = owner + bit - 2 * bit * (rank // bit % 2)
        return left_refs[part].at[pl.ds(pl.multiple_of(owner * block, block), block)]

    def by_columns(function):
        @pl.loop(0, width // stride)
        def _(step):
            function(pl.ds(pl.multiple_of(step * stride, stride), stride))

    core_copies = {}
    ring_copies = {}
    slot = 0
    plan = scatter_plan(bits, parts)
    for part, bit, moved in plan:
        for pattern in moved:
            ring_copies[part, bit, pattern] = (
                slot,
                pltpu.make_async_remote_copy(
                    src_ref=held.at[part, place[pattern]],
                    dst_ref=passed.at[slot],
                    send_sem=ring_send.at[slot],
                    recv_sem=ring_recv.at[slot],
                    device_id={"dp": across(bit)},
                    device_id_type=pl.DeviceIdType.MESH,
                ),
            )
            slot += 1

    def far_tile(part, pattern):
        rows = tile_rows(part, pattern | 1)
        index = part * len(patterns) + place[pattern]

        def columns(window):
            far[index, :, window] = jnp.dot(
                rows[...], right_ref[:, window], preferred_element_type=WIDE
            ).astype(LOW)

        by_columns(columns)
        copy = pltpu.make_async_remote_copy(
            src_ref=far.at[index],
            dst_ref=arrived.at[index],
            send_sem=core_send.at[index],
            recv_sem=core_recv.at[index],
            device_id={"dp": across(1)},
            device_id_type=pl.DeviceIdType.MESH,
        )
        copy.start()
        core_copies[part, pattern] = (index, copy)

    def near_tile(part, pattern):
        rows = tile_rows(part, pattern)
        index, copy = core_copies[part, pattern]
        copy.wait_recv()

        def columns(window):
            value = jnp.dot(
                rows[...], right_ref[:, window], preferred_element_type=WIDE
            ) + arrived[index, :, window].astype(WIDE)
            if pattern:
                held[part, place[pattern], :, window] = value.astype(LOW)
            else:
                out_ref[part, :, window] = value

        by_columns(columns)

    def send(part, bit, moved):
        for pattern in moved:
            ring_copies[part, bit, pattern][1].start()

    def take(part, bit, moved):
        for pattern in moved:
            number, copy = ring_copies[part, bit, pattern]
            copy.wait_recv()
            target = pattern - bit

            def columns(window):
                coming = passed[number, :, window].astype(WIDE)
                if target:
                    old = held[part, place[target], :, window].astype(WIDE)
                    held[part, place[target], :, window] = (old + coming).astype(LOW)
                else:
                    out_ref[part, :, window] = out_ref[part, :, window] + coming

            by_columns(columns)

    steps = [[entry for entry in plan if entry[0] == part] for part in range(parts)]
    first = [steps[part][0] for part in range(parts)]
    urgent = [
        (part, pattern)
        for tiles in zip(*[sorted(entry[2], reverse=True) for entry in first])
        for part, pattern in enumerate(tiles)
    ]
    others = [
        (part, pattern)
        for pattern in sorted(patterns, reverse=True)
        for part in range(parts)
        if (part, pattern) not in urgent
    ]
    queue = urgent + others
    ahead = 2 * parts
    for entry in queue[:ahead]:
        far_tile(*entry)
    for number, (part, pattern) in enumerate(queue):
        near_tile(part, pattern)
        if (part, pattern) in urgent:
            ring_copies[part, first[part][1], pattern][1].start()
        if number + ahead < len(queue):
            far_tile(*queue[number + ahead])
    for level in range(len(bits)):
        for part in range(parts):
            take(*steps[part][level])
            if level + 1 < len(bits):
                send(*steps[part][level + 1])
    for _, copy in list(core_copies.values()) + list(ring_copies.values()):
        copy.wait_send()


def product_scatter(lefts, right, collective_id):
    parts = len(lefts)
    plane = lax.axis_size("dp")
    bits = [1 << k for k in range(1, plane.bit_length() - 1)]
    rows, depth = lefts[0].shape
    width = right.shape[1]
    block = rows // plane
    tiles = plane // 2
    passes = sum(len(moved) for _, _, moved in scatter_plan(bits, parts))
    sent = parts * tiles * block * width * 2 * 2
    result = pl.pallas_call(
        functools.partial(scatter_kernel, bits, parts),
        out_shape=jax.ShapeDtypeStruct((parts, block, width), WIDE),
        in_specs=[pl.BlockSpec(memory_space=pltpu.VMEM)] * (parts + 1),
        out_specs=pl.BlockSpec(memory_space=pltpu.VMEM),
        scratch_shapes=[
            pltpu.VMEM((parts * tiles, block, width), LOW),
            pltpu.VMEM((parts * tiles, block, width), LOW),
            pltpu.VMEM((parts, tiles, block, width), LOW),
            pltpu.VMEM((passes, block, width), LOW),
            pltpu.SemaphoreType.DMA((parts * tiles,)),
            pltpu.SemaphoreType.DMA((parts * tiles,)),
            pltpu.SemaphoreType.DMA((passes,)),
            pltpu.SemaphoreType.DMA((passes,)),
        ],
        cost_estimate=pl.CostEstimate(
            flops=2 * parts * rows * depth * width,
            bytes_accessed=8 * sent,
            transcendentals=0,
        ),
        compiler_params=pltpu.CompilerParams(
            collective_id=collective_id, has_side_effects=True, vmem_limit_bytes=60 << 20
        ),
        name="product_scatter",
    )(*lefts, right)
    return [result[b] for b in range(parts)]


ROOT = (2.0 / 3.141592653589793) ** 0.5


def gelu_slope(values_in):
    squared = values_in * values_in
    bend = jnp.tanh(ROOT * values_in * (1.0 + 0.044715 * squared))
    slope = ROOT * (1.0 + 3.0 * 0.044715 * squared)
    return 0.5 * (1.0 + bend) + 0.5 * values_in * (1.0 - bend * bend) * slope


def gather_kernel(bits, parts, mode, *refs):
    backward, plain = mode == "slope", mode == "plain"
    block_refs = refs[:parts]
    weight_ref = refs[parts]
    rest = refs[parts + 1 :]
    if backward:
        wide_refs, rest = rest[:parts], rest[parts:]
        gathered_refs, low_refs, rest = rest[:parts], rest[parts : 2 * parts], rest[2 * parts :]
    elif plain:
        wide_refs = None
        gathered_refs, low_refs, rest = rest[:parts], rest[parts : 2 * parts], rest[2 * parts :]
    else:
        bias_ref, rest = rest[0], rest[1:]
        gathered_refs, wide_refs = rest[:parts], rest[parts : 2 * parts]
        low_refs, rest = rest[2 * parts : 3 * parts], rest[3 * parts :]
    landed, wide_stage, low_stage = rest[:3]
    send_sems, recv_sems, keep_sems, wide_sems, low_sems = rest[3:]
    rank = lax.axis_index("dp")
    block = block_refs[0].shape[0]
    hidden = weight_ref.shape[0]
    stride = min(512, hidden)

    def across(bit):
        return rank + bit - 2 * bit * (rank // bit % 2)

    barrier = pltpu.get_barrier_semaphore()
    partners = [1] + list(bits)
    for bit in partners:
        pl.semaphore_signal(
            barrier,
            inc=1,
            device_id={"dp": across(bit)},
            device_id_type=pl.DeviceIdType.MESH,
        )
    pl.semaphore_wait(barrier, len(partners))

    plane = 1 << len(partners)
    orders = [list(bits) if part % 2 == 0 else list(bits)[::-1] for part in range(parts)]
    near = [patterns_of(order) for order in orders]
    copies = {}

    def slot(part, pattern):
        return part * plane + pattern

    def source(part, pattern):
        return landed.at[slot(part, pattern)] if pattern else block_refs[part]

    def pass_on(part, pattern, bit):
        target = slot(part, pattern | bit)
        copy = pltpu.make_async_remote_copy(
            src_ref=source(part, pattern),
            dst_ref=landed.at[target],
            send_sem=send_sems.at[target],
            recv_sem=recv_sems.at[target],
            device_id={"dp": across(bit)},
            device_id_type=pl.DeviceIdType.MESH,
        )
        copy.start()
        copies[part, pattern | bit] = copy

    def place_of(pattern):
        owner = rank
        for bit in partners:
            if pattern & bit:
                owner = owner + bit - 2 * bit * (rank // bit % 2)
        return pl.ds(pl.multiple_of(owner * block, block), block)

    kept = []

    def keep(part, pattern):
        copy = pltpu.make_async_copy(
            source(part, pattern),
            gathered_refs[part].at[place_of(pattern)],
            keep_sems.at[slot(part, pattern)],
        )
        copy.start()
        kept.append(copy)

    sequence = []
    for turn in range(len(near[0])):
        sequence += [(part, near[part][turn]) for part in range(parts)]
        sequence += [(part, near[part][turn] | 1) for part in range(parts)]
    stored = {}

    def fetch(number):
        part, pattern = sequence[number]
        copy = pltpu.make_async_copy(
            wide_refs[part].at[place_of(pattern)],
            wide_stage.at[number % 2],
            wide_sems.at[number % 2],
        )
        copy.start()
        return copy

    def multiply(number):
        part, pattern = sequence[number]
        turn = number % 2
        rows = source(part, pattern)
        for copy in stored.pop(number - 2, ()):
            copy.wait()
        if backward:
            stored_wide.pop(number).wait()

        @pl.loop(0, hidden // stride)
        def _(step):
            window = pl.ds(pl.multiple_of(step * stride, stride), stride)
            product = contract(rows[...], weight_ref[window], 1, 1)
            if backward:
                value = product * gelu_slope(wide_stage[turn, :, window])
            elif plain:
                value = product
            else:
                value = product + bias_ref[:, window]
                wide_stage[turn, :, window] = value
                value = gelu_tanh(value)
            low_stage[turn, :, window] = value.astype(LOW)

        if backward and number + 2 < len(sequence):
            stored_wide[number + 2] = fetch(number + 2)
        outgoing = [
            pltpu.make_async_copy(
                low_stage.at[turn], low_refs[part].at[place_of(pattern)], low_sems.at[turn]
            )
        ]
        if not backward and not plain:
            outgoing.append(
                pltpu.make_async_copy(
                    wide_stage.at[turn], wide_refs[part].at[place_of(pattern)], wide_sems.at[turn]
                )
            )
        for copy in outgoing:
            copy.start()
        stored[number] = outgoing

    stored_wide = {}
    if backward:
        for number in range(2):
            stored_wide[number] = fetch(number)
    for turn in range(len(bits)):
        for part in range(parts):
            pass_on(part, 0, orders[part][turn])
    for part in range(parts):
        pass_on(part, 0, 1)
        keep(part, 0)

    number = 0
    for turn in range(len(near[0])):
        if turn:
            for part in range(parts):
                pattern = near[part][turn]
                copies[part, pattern].wait_recv()
                highest = max(orders[part].index(bit) for bit in bits if pattern & bit)
                for bit in orders[part][highest + 1 :]:
                    pass_on(part, pattern, bit)
                pass_on(part, pattern, 1)
                keep(part, pattern)
        for part in range(parts):
            multiply(number)
            number += 1
        for part in range(parts):
            pattern = near[part][turn] | 1
            copies[part, pattern].wait_recv()
            keep(part, pattern)
            multiply(number)
            number += 1
    for outgoing in stored.values():
        for copy in outgoing:
            copy.wait()
    for copy in kept:
        copy.wait()
    for copy in copies.values():
        copy.wait_send()


def gather_product(blocks, weight, extra, collective_id):
    mode = "plain" if extra is None else "slope" if isinstance(extra, list) else "bias"
    parts = len(blocks)
    plane = lax.axis_size("dp")
    bits = [1 << k for k in range(1, plane.bit_length() - 1)]
    block, width = blocks[0].shape
    hidden = weight.shape[0]
    rows = plane * block
    vmem, anywhere = (
        pl.BlockSpec(memory_space=pltpu.VMEM),
        pl.BlockSpec(memory_space=pl.ANY),
    )
    gathered = jax.ShapeDtypeStruct((rows, width), LOW)
    wide = jax.ShapeDtypeStruct((rows, hidden), WIDE)
    low = jax.ShapeDtypeStruct((rows, hidden), LOW)
    outs = [gathered] * parts + ([wide] * parts if mode == "bias" else []) + [low] * parts
    extras = {"plain": [], "bias": [extra], "slope": extra}[mode]
    results = pl.pallas_call(
        functools.partial(gather_kernel, bits, parts, mode),
        out_shape=outs,
        in_specs=[vmem] * (parts + 1) + [anywhere if mode == "slope" else vmem] * len(extras),
        out_specs=[anywhere] * len(outs),
        scratch_shapes=[
            pltpu.VMEM((parts * plane, block, width), LOW),
            pltpu.VMEM((2, block, hidden), WIDE),
            pltpu.VMEM((2, block, hidden), LOW),
            pltpu.SemaphoreType.DMA((parts * plane,)),
            pltpu.SemaphoreType.DMA((parts * plane,)),
            pltpu.SemaphoreType.DMA((parts * plane,)),
            pltpu.SemaphoreType.DMA((2,)),
            pltpu.SemaphoreType.DMA((2,)),
        ],
        cost_estimate=pl.CostEstimate(
            flops=2 * parts * rows * hidden * width,
            bytes_accessed=16 * parts * rows * width,
            transcendentals=parts * rows * hidden,
        ),
        compiler_params=pltpu.CompilerParams(
            collective_id=collective_id, has_side_effects=True, vmem_limit_bytes=60 << 20
        ),
        name="gather_product",
    )(*blocks, weight, *extras)
    return [list(results[k : k + parts]) for k in range(0, len(outs), parts)]


def opening_kernel(bits, parts, depth, *refs):
    block_refs, piece_ref = refs[:parts], refs[parts]
    gathered_refs, line_ref = refs[parts + 1 : 2 * parts + 1], refs[2 * parts + 1]
    landed, held_line = refs[2 * parts + 2 : 2 * parts + 4]
    send_sems, recv_sems, keep_sems, line_send, line_recv, line_keep = refs[2 * parts + 4 :]
    rank, level = lax.axis_index("dp"), lax.axis_index("mp")
    block = block_refs[0].shape[0]

    def across(bit):
        return rank + bit - 2 * bit * (rank // bit % 2)

    partners = [1] + list(bits)
    plane = 1 << len(partners)
    barrier = pltpu.get_barrier_semaphore()
    for bit in partners:
        pl.semaphore_signal(
            barrier,
            inc=1,
            device_id={"dp": across(bit)},
            device_id_type=pl.DeviceIdType.MESH,
        )
    for shift in (1, depth - 1):
        pl.semaphore_signal(
            barrier,
            inc=1,
            device_id={"mp": (level + shift) % depth},
            device_id_type=pl.DeviceIdType.MESH,
        )
    pl.semaphore_wait(barrier, len(partners) + 2)

    def line_copy(up, step):
        shard = level - step if up else level + step
        number = step * 2 + (0 if up else 1)
        return pltpu.make_async_remote_copy(
            src_ref=held_line.at[shard] if step else piece_ref,
            dst_ref=held_line.at[shard],
            send_sem=line_send.at[number],
            recv_sem=line_recv.at[number],
            device_id={"mp": (level + (1 if up else depth - 1)) % depth},
            device_id_type=pl.DeviceIdType.MESH,
        )

    def sends(up, step):
        if up:
            return jnp.logical_and(level + 1 < depth, level >= step)
        return jnp.logical_and(level > 0, level + step < depth)

    def receives(up, step):
        return level > step if up else level + step + 1 < depth

    orders = [list(bits) if part % 2 == 0 else list(bits)[::-1] for part in range(parts)]
    near = [patterns_of(order) for order in orders]
    copies = {}

    def place_of(pattern):
        owner = rank
        for bit in partners:
            if pattern & bit:
                owner = owner + bit - 2 * bit * (rank // bit % 2)
        return pl.ds(pl.multiple_of(owner * block, block), block)

    def pass_on(part, pattern, bit):
        target = part * plane + (pattern | bit)
        copy = pltpu.make_async_remote_copy(
            src_ref=landed.at[part * plane + pattern] if pattern else block_refs[part],
            dst_ref=landed.at[target],
            send_sem=send_sems.at[target],
            recv_sem=recv_sems.at[target],
            device_id={"dp": across(bit)},
            device_id_type=pl.DeviceIdType.MESH,
        )
        copy.start()
        copies[part, pattern | bit] = copy

    def line_start(step):
        for up in (True, False):

            @pl.when(sends(up, step))
            def _():
                line_copy(up, step).start()

    line_start(0)
    for turn in range(len(bits)):
        for part in range(parts):
            pass_on(part, 0, orders[part][turn])
    kept = []

    def keep(part, pattern):
        number = part * plane + pattern
        copy = pltpu.make_async_copy(
            landed.at[number] if pattern else block_refs[part],
            gathered_refs[part].at[place_of(pattern)],
            keep_sems.at[number],
        )
        copy.start()
        kept.append(copy)

    def line_keep_copy(up, step):
        shard = level - step if up else level + step
        return pltpu.make_async_copy(
            held_line.at[shard] if step else piece_ref,
            line_ref.at[shard],
            line_keep.at[step * 2 - (0 if up else 1)],
        )

    for part in range(parts):
        pass_on(part, 0, 1)
        keep(part, 0)
    line_keep_copy(True, 0).start()
    for turn in range(1, max(len(near[0]), depth)):
        if turn < len(near[0]):
            for part in range(parts):
                pattern = near[part][turn]
                copies[part, pattern].wait_recv()
                highest = max(orders[part].index(bit) for bit in bits if pattern & bit)
                for bit in orders[part][highest + 1 :]:
                    pass_on(part, pattern, bit)
                pass_on(part, pattern, 1)
                keep(part, pattern)
        if turn < depth:
            for up in (True, False):

                @pl.when(receives(up, turn - 1))
                def _():
                    line_copy(up, turn - 1).wait_recv()
                    line_keep_copy(up, turn).start()

            if turn < depth - 1:
                line_start(turn)
    for part in range(parts):
        for pattern in near[part]:
            copies[part, pattern | 1].wait_recv()
            keep(part, pattern | 1)
    for copy in kept:
        copy.wait()
    for copy in copies.values():
        copy.wait_send()
    line_keep_copy(True, 0).wait()
    for step in range(depth - 1):
        for up in (True, False):

            @pl.when(receives(up, step))
            def _():
                line_keep_copy(up, step + 1).wait()

            @pl.when(sends(up, step))
            def _():
                line_copy(up, step).wait_send()


def opening_gather(blocks, piece, collective_id):
    parts = len(blocks)
    plane, depth = lax.axis_size("dp"), lax.axis_size("mp")
    bits = [1 << k for k in range(1, plane.bit_length() - 1)]
    block, width = blocks[0].shape
    anywhere = pl.BlockSpec(memory_space=pl.ANY)
    results = pl.pallas_call(
        functools.partial(opening_kernel, bits, parts, depth),
        out_shape=[jax.ShapeDtypeStruct((plane * block, width), LOW)] * parts
        + [jax.ShapeDtypeStruct((depth,) + piece.shape, LOW)],
        in_specs=[pl.BlockSpec(memory_space=pltpu.VMEM)] * (parts + 1),
        out_specs=[anywhere] * (parts + 1),
        scratch_shapes=[
            pltpu.VMEM((parts * plane, block, width), LOW),
            pltpu.VMEM((depth,) + piece.shape, LOW),
            pltpu.SemaphoreType.DMA((parts * plane,)),
            pltpu.SemaphoreType.DMA((parts * plane,)),
            pltpu.SemaphoreType.DMA((parts * plane,)),
            pltpu.SemaphoreType.DMA((2 * (depth - 1),)),
            pltpu.SemaphoreType.DMA((2 * (depth - 1),)),
            pltpu.SemaphoreType.DMA((2 * depth - 1,)),
        ],
        cost_estimate=pl.CostEstimate(
            flops=0, bytes_accessed=16 * parts * plane * block * width, transcendentals=0
        ),
        compiler_params=pltpu.CompilerParams(
            collective_id=collective_id, has_side_effects=True, vmem_limit_bytes=60 << 20
        ),
        name="opening_gather",
    )(*blocks, piece)
    return list(results[:parts]), results[parts]


def sum_over(axes, vector):
    for axis in axes:
        size = lax.axis_size(axis)
        step = 1
        while step < size:
            vector = vector + lax.ppermute(vector, axis, [(k, k ^ step) for k in range(size)])
            step *= 2
    return vector


def body(
    inputs,
    segment_ids,
    cotangent,
    query_weight,
    key_weight,
    value_weight,
    out_weight,
    up_weight,
    down_weight,
    query_bias,
    value_bias,
    out_bias,
    up_bias,
    down_bias,
    first_gain,
    first_shift,
    second_gain,
    second_shift,
):
    plane, depth = lax.axis_size("dp"), lax.axis_size("mp")
    rank, level = lax.axis_index("dp"), lax.axis_index("mp")
    parts, block, width = inputs.shape
    length = block * depth
    group = depth // parts
    seqs = plane // group
    rows = group * block
    hidden = up_bias.shape[0] // plane
    heads_in_block = query_weight.shape[1] // HEAD_DIM
    sharers = plane // heads_in_block
    heads = depth // sharers
    parity = level % parts

    def route(turn, back):
        pairs = []
        for i in range(plane):
            for j in range(depth):
                e = (j + turn) % parts
                source = i * depth + j
                target = (i - i % group + j // parts) * depth + parts * (i % group) + e
                pairs.append((target, source) if back else (source, target))
        return pairs

    def pick(options, index):
        return lax.dynamic_index_in_dim(jnp.stack(options), index % parts, 0, keepdims=False)

    def enter(array):
        arrived = [
            lax.ppermute(
                lax.dynamic_index_in_dim(array, (level + turn) % parts, 0, keepdims=False),
                ("dp", "mp"),
                route(turn, False),
            )
            for turn in range(parts)
        ]
        return [pick(arrived, parity - b + parts) for b in range(parts)]

    def leave_picks(blocks):
        return [pick(blocks, parity - turn + parts) for turn in range(parts)]

    def leave_sent(picks):
        return [
            lax.ppermute(picks[turn], ("dp", "mp"), route(turn, True)) for turn in range(parts)
        ]

    def leave_placed(arrived):
        return jnp.stack([pick(arrived, e - parity + parts) for e in range(parts)])

    def gather(array):
        return lax.all_gather(array, "dp", axis=0, tiled=True)

    def gather_in_order(arrays):
        return [gather(array) for array in together(arrays)]

    def swap(array, bit):
        return lax.ppermute(array, "dp", [(k, k ^ bit) for k in range(plane)])

    bits = [1 << k for k in range(plane.bit_length() - 1)]

    sharing = [list(range(k, k + sharers)) for k in range(0, plane, sharers)]

    def share_out(array):
        if sharers == 1:
            return array
        return lax.all_to_all(
            array, "dp", split_axis=0, concat_axis=2, axis_index_groups=sharing, tiled=True
        )

    def share_back(array):
        if sharers == 1:
            return array
        return lax.all_to_all(
            array, "dp", split_axis=2, concat_axis=0, axis_index_groups=sharing, tiled=True
        )

    tokens = enter(inputs)
    attention_shards = jnp.stack([query_weight.T, key_weight.T, value_weight.T, out_weight])
    attention_shards = attention_shards.reshape(4, plane, -1, width // plane)
    attention_pieces = lax.all_to_all(
        attention_shards.transpose(1, 0, 2, 3).reshape(-1, width // plane),
        "dp",
        split_axis=0,
        concat_axis=1,
        tiled=True,
    )
    segments = segment_ids
    for bit in bits:
        other = swap(segments, bit)
        upper = rank // bit % 2 == 1
        segments = jnp.concatenate(
            [jnp.where(upper, other, segments), jnp.where(upper, segments, other)]
        )
    segments = lax.dynamic_index_in_dim(
        segments.reshape(seqs, depth, length), level, 1, keepdims=False
    )
    segments = segments.reshape(seqs, group, parts, block).transpose(0, 2, 1, 3)
    segment_rows = segments.reshape(seqs, parts, rows)
    segment_cols = segments.reshape(seqs, parts * rows, 1)
    tokens, segment_rows, segment_cols = together((tokens, segment_rows, segment_cols))
    gathered_inputs, attention_line = opening_gather(tokens, attention_pieces, 7)
    attention_full = share_out(attention_line.reshape(depth, 4, -1, width))
    forward_shards, attention_full = together(((up_weight.T, down_weight), attention_full))
    up_piece, down_piece = [
        lax.all_to_all(shard, "dp", split_axis=0, concat_axis=1, tiled=True)
        for shard in forward_shards
    ]
    attention_full = attention_full.transpose(1, 0, 2, 3).reshape(4, heads * HEAD_DIM, width)
    full_qkv = attention_full[:3].reshape(3 * heads * HEAD_DIM, width)
    full_out = attention_full[3]
    def own_heads(bias):
        table = bias.reshape(depth, heads_in_block, HEAD_DIM)
        return lax.dynamic_slice(
            table, (rank % sharers * heads, rank // sharers, 0), (heads, 1, HEAD_DIM)
        ).reshape(-1)

    qkv_bias = jnp.concatenate(
        [own_heads(query_bias), jnp.zeros((heads * HEAD_DIM,), WIDE), own_heads(value_bias)]
    )
    own_up = lax.dynamic_slice(
        up_bias.reshape(depth, plane, -1), (0, rank, 0), (depth, 1, hidden // depth)
    ).reshape(-1)

    every = range(parts)
    qkv = [
        (contract(gathered_inputs[b], full_qkv, 1, 1) + qkv_bias).astype(LOW) for b in every
    ]
    full_up = lax.all_gather(up_piece, "mp", axis=0, tiled=True)
    full_down = lax.all_gather(down_piece, "mp", axis=0, tiled=True)
    cotangent, qkv = together((cotangent, qkv))
    tangents = enter(cotangent)
    attended, lses = [], []
    for b in every:
        mixed, lse = attend_forward(b, qkv, segment_cols, segment_rows)
        attended.append(mixed)
        lses.append(lse)
    attn_sums = product_scatter(attended, full_out, 1)
    first = [
        norm_forward(tokens[b].astype(WIDE) + attn_sums[b] + out_bias, first_gain, first_shift)
        for b in every
    ]
    first_low = [first[b][0].astype(LOW) for b in every]
    first_low, full_up, full_down = together((first_low, full_up, full_down))
    gathered_first, up_proj, hiddens = gather_product(
        first_low, full_up, own_up.reshape(1, -1), 4
    )
    hiddens, tangents = together((hiddens, tangents))
    tangents = [array.astype(WIDE) for array in tangents]
    ffn_sums = product_scatter(hiddens, full_down, 2)
    second = [
        norm_forward(first[b][0] + ffn_sums[b] + down_bias, second_gain, second_shift)
        for b in every
    ]
    outputs = leave_placed(
        leave_sent(leave_picks([second[b][0].astype(LOW) for b in every]))
    )

    def share_attention(term):
        return share_back(term.reshape(-1, heads, HEAD_DIM, width).transpose(1, 0, 2, 3))

    def reduce_attention(term):
        return lax.psum_scatter(share_attention(term), "mp", scatter_dimension=0, tiled=True)[0]

    def reduce_forward(term):
        return lax.psum_scatter(term, "mp", scatter_dimension=0, tiled=True)

    def owner_exchange(term):
        return lax.all_to_all(
            term.reshape(-1, width), "dp", split_axis=1, concat_axis=0, tiled=True
        )

    def low_sum(terms):
        return sum(terms).astype(LOW)

    def total(arrays):
        return sum(jnp.sum(array.astype(WIDE), axis=0) for array in arrays)

    grad_second_gain = total([tangents[b] * second[b][1] for b in every])
    grad_second_shift = total(tangents)
    grad_two = [
        norm_backward(tangents[b], second[b][1], second[b][2], second_gain) for b in every
    ]
    grad_ffn = [array.astype(LOW) for array in grad_two]
    grad_down_bias = total(grad_ffn)
    gathered_ffn, grad_upper = gather_product(grad_ffn, full_down, up_proj, 5)
    gathered_ffn, grad_upper, outputs = together((gathered_ffn, grad_upper, outputs))
    grad_up_bias = total(grad_upper)
    back_sums = product_scatter(grad_upper, full_up, 2)
    term_down = low_sum(contract(hiddens[b], gathered_ffn[b], 0, 0) for b in every)
    term_up = low_sum(contract(grad_upper[b], gathered_first[b], 0, 0) for b in every)
    grad_first = [grad_two[b] + back_sums[b] for b in every]
    grad_first_gain = total([grad_first[b] * first[b][1] for b in every])
    grad_first_shift = total(grad_first)
    grad_resid = [
        norm_backward(grad_first[b], first[b][1], first[b][2], first_gain) for b in every
    ]
    grad_branch = [array.astype(LOW) for array in grad_resid]
    reduced_down = reduce_forward(term_down)
    grad_branch, reduced_down = together((grad_branch, reduced_down))
    grad_out_bias = total(grad_branch)
    gathered_branch, grad_mixed = gather_product(grad_branch, full_out, None, 6)
    spread_up = lax.dynamic_update_slice(
        jnp.zeros((depth, plane, hidden // depth), WIDE),
        grad_up_bias.reshape(depth, 1, -1),
        (0, rank, 0),
    ).reshape(-1)
    owned_down = owner_exchange(reduced_down)
    reduced_up = reduce_forward(term_up)
    grad_mixed = [
        array.reshape(seqs * rows, heads * HEAD_DIM)
        for array in together((grad_mixed, term_up))[0]
    ]
    grad_qkv, grad_qkv_bias = attend_backward(qkv, grad_mixed, lses, segment_cols, segment_rows)

    def spread_heads(piece):
        table = jnp.zeros((depth, heads_in_block, HEAD_DIM), WIDE)
        return lax.dynamic_update_slice(
            table,
            piece.reshape(heads, 1, HEAD_DIM),
            (rank % sharers * heads, rank // sharers, 0),
        ).reshape(-1)

    spread = heads * HEAD_DIM
    vectors = jnp.concatenate(
        [
            spread_heads(grad_qkv_bias[:spread]),
            spread_heads(grad_qkv_bias[2 * spread :]),
            grad_out_bias,
            grad_down_bias,
            grad_first_gain,
            grad_first_shift,
            grad_second_gain,
            grad_second_shift,
            spread_up,
        ]
    )
    vectors = sum_over(("mp",), vectors.reshape(-1, HEAD_DIM))
    reduced_out = reduce_attention(
        low_sum(contract(attended[b], gathered_branch[b], 0, 0) for b in every)
    )
    term_qkv = low_sum(contract(grad_qkv[b], gathered_inputs[b], 0, 0) for b in every)
    term_qkv, reduced_up = together((term_qkv, reduced_up))
    shared_qkv = share_attention(term_qkv)
    owned_up = owner_exchange(reduced_up)
    grad_qkv, shared_qkv, vectors = together((grad_qkv, shared_qkv, vectors))
    input_sums = product_scatter(grad_qkv, full_qkv, 3)
    reduced_qkv = lax.psum_scatter(shared_qkv, "mp", scatter_dimension=0, tiled=True)[0]
    grad_low = [(grad_resid[b] + input_sums[b]).astype(LOW) for b in every]
    leaving = leave_sent(leave_picks(grad_low))
    vectors = sum_over(("dp",), vectors).reshape(-1)
    grad_inputs = leave_placed(leaving).astype(WIDE)

    owned_out = owner_exchange(reduced_out)
    owned_qkv = owner_exchange(reduced_qkv)
    owned_qkv = owned_qkv.reshape(plane, 3, -1, width // plane).transpose(1, 0, 2, 3)
    owned_qkv = owned_qkv.reshape(3, -1, width // plane)

    narrow = vectors[: 8 * width].reshape(8, width)
    return (
        outputs,
        grad_inputs,
        owned_qkv[0].T.astype(WIDE),
        owned_qkv[1].T.astype(WIDE),
        owned_qkv[2].T.astype(WIDE),
        owned_out.astype(WIDE),
        owned_up.T.astype(WIDE),
        owned_down.astype(WIDE),
        narrow[0],
        narrow[1],
        narrow[2],
        vectors[8 * width :],
        narrow[3],
        narrow[4],
        narrow[5],
        narrow[6],
        narrow[7],
    )


def solution(mesh):
    tokens = P("dp", "mp", None)
    by_rows, by_columns, whole = P("dp", "mp"), P("mp", "dp"), P()
    in_specs = (
        (tokens, P("dp", None), tokens)
        + (by_rows,) * 3
        + (by_columns, by_rows, by_columns)
        + (whole,) * 9
    )
    out_specs = (
        (tokens, tokens) + (by_rows,) * 3 + (by_columns, by_rows, by_columns) + (whole,) * 9
    )
    return jax.shard_map(body, mesh=mesh, in_specs=in_specs, out_specs=out_specs, check_vma=False)
```

```python
import functools

import jax
import jax.numpy as jnp
from jax import lax
from jax.experimental import pallas as pl
from jax.experimental.pallas import tpu as pltpu
from jax.sharding import PartitionSpec as P


HEAD_DIM = 128
SCALING = HEAD_DIM ** (-0.5)
EPSILON = 1e-12
MASKED = -1e30
LOW = jnp.bfloat16
WIDE = jnp.float32


def contract(left, right, left_dim, right_dim):
    return lax.dot_general(
        left, right, (((left_dim,), (right_dim,)), ((), ())), preferred_element_type=WIDE
    )


def norm_forward(resid, scale_vec, shift_vec):
    average = jnp.mean(resid, axis=-1, keepdims=True)
    centered = resid - average
    variance = jnp.mean(centered * centered, axis=-1, keepdims=True)
    inv_std = lax.rsqrt(variance + EPSILON)
    normed = centered * inv_std
    return normed * scale_vec + shift_vec, normed, inv_std


def norm_backward(upstream, normed, inv_std, scale_vec):
    scaled = upstream * scale_vec
    first_mean = jnp.mean(scaled, axis=-1, keepdims=True)
    second_mean = jnp.mean(scaled * normed, axis=-1, keepdims=True)
    return inv_std * (scaled - first_mean - normed * second_mean)


def gelu_tanh(values_in):
    return jax.nn.gelu(values_in, approximate=True)


def head_rows(refs, column):
    return jnp.concatenate([ref[:, column : column + HEAD_DIM] for ref in refs], axis=0)


def forward_kernel(heads, parts, which, *refs):
    qkv_refs = refs[:parts]
    keys_segment, query_segments, out_ref, lse_ref = refs[parts:]
    segment_col = keys_segment[0]
    segment_row = query_segments[0, which : which + 1]
    allowed = segment_col == segment_row
    for head in range(heads):
        queries = qkv_refs[which][:, head * HEAD_DIM : (head + 1) * HEAD_DIM]
        keys_all = head_rows(qkv_refs, (heads + head) * HEAD_DIM)
        values_all = head_rows(qkv_refs, (2 * heads + head) * HEAD_DIM)
        logits = jnp.where(allowed, contract(keys_all, queries, 1, 1) * SCALING, MASKED)
        top = jnp.max(logits, axis=0, keepdims=True)
        expo = jnp.exp(logits - top)
        total = jnp.sum(expo, axis=0, keepdims=True)
        probs_low = (expo * (1.0 / total)).astype(LOW)
        mixed = contract(values_all, probs_low, 0, 0)
        out_ref[:, head * HEAD_DIM : (head + 1) * HEAD_DIM] = mixed.T.astype(LOW)
        lse_ref[0, head : head + 1] = top + jnp.log(total)


def backward_kernel(heads, parts, *refs):
    qkv_refs = refs[:parts]
    grad_refs = refs[parts : 2 * parts]
    lse_refs = refs[2 * parts : 3 * parts]
    keys_segment, query_segments = refs[3 * parts : 3 * parts + 2]
    out_refs = refs[3 * parts + 2 : 4 * parts + 2]
    bias_ref = refs[4 * parts + 2]
    rows = qkv_refs[0].shape[0]
    segment_col = keys_segment[0]
    bias_ref[...] = jnp.zeros_like(bias_ref)
    for head in range(heads):
        base = head * HEAD_DIM
        keys_all = head_rows(qkv_refs, heads * HEAD_DIM + base)
        values_all = head_rows(qkv_refs, 2 * heads * HEAD_DIM + base)
        grad_keys = 0.0
        grad_values = 0.0
        query_bias = 0.0
        for which in range(parts):
            queries = qkv_refs[which][:, base : base + HEAD_DIM]
            grad_mixed = grad_refs[which][:, base : base + HEAD_DIM]
            allowed = segment_col == query_segments[0, which : which + 1]
            logits = contract(keys_all, queries, 1, 1) * SCALING
            probs = jnp.where(allowed, jnp.exp(logits - lse_refs[which][0, head : head + 1]), 0.0)
            grad_probs = contract(values_all, grad_mixed, 1, 1)
            inner = jnp.sum(probs * grad_probs, axis=0, keepdims=True)
            grad_logits = (probs * (grad_probs - inner)).astype(LOW)
            probs_low = probs.astype(LOW)
            grad_values = grad_values + jnp.dot(
                probs_low, grad_mixed, preferred_element_type=WIDE
            )
            grad_keys = grad_keys + jnp.dot(grad_logits, queries, preferred_element_type=WIDE)
            grad_queries = (contract(keys_all, grad_logits, 0, 0) * SCALING).T.astype(LOW)
            query_bias = query_bias + jnp.sum(grad_queries.astype(WIDE), axis=0, keepdims=True)
            out_refs[which][:, base : base + HEAD_DIM] = grad_queries
        grad_keys = (grad_keys * SCALING).astype(LOW)
        grad_values = grad_values.astype(LOW)
        bias_ref[0, :, base : base + HEAD_DIM] = query_bias
        start = 2 * heads * HEAD_DIM + base
        bias_ref[0, :, start : start + HEAD_DIM] = jnp.sum(
            grad_values.astype(WIDE), axis=0, keepdims=True
        )
        for which in range(parts):
            piece = slice(which * rows, (which + 1) * rows)
            start = heads * HEAD_DIM + base
            out_refs[which][:, start : start + HEAD_DIM] = grad_keys[piece]
            start = 2 * heads * HEAD_DIM + base
            out_refs[which][:, start : start + HEAD_DIM] = grad_values[piece]


def row_spec(rows, width):
    return pl.BlockSpec((rows, width), lambda s: (s, 0))


def cube_spec(*dims):
    return pl.BlockSpec((1,) + dims, lambda s: (s, 0, 0))


def attend_forward(which, qkv, segment_cols, segment_rows):
    parts = len(qkv)
    seqs, _, rows = segment_rows.shape
    width = qkv[0].shape[1] // 3
    heads = width // HEAD_DIM
    pairs = seqs * heads * rows * rows * parts
    return pl.pallas_call(
        functools.partial(forward_kernel, heads, parts, which),
        grid=(seqs,),
        in_specs=[row_spec(rows, 3 * width)] * parts
        + [cube_spec(parts * rows, 1), cube_spec(parts, rows)],
        out_specs=[row_spec(rows, width), cube_spec(heads, rows)],
        out_shape=[
            jax.ShapeDtypeStruct((seqs * rows, width), LOW),
            jax.ShapeDtypeStruct((seqs, heads, rows), WIDE),
        ],
        cost_estimate=pl.CostEstimate(
            flops=4 * pairs * HEAD_DIM,
            bytes_accessed=8 * seqs * rows * width * parts,
            transcendentals=pairs,
        ),
        compiler_params=pltpu.CompilerParams(vmem_limit_bytes=56 << 20),
        name="attend_forward",
    )(*qkv, segment_cols, segment_rows)


def attend_backward(qkv, grads, lses, segment_cols, segment_rows):
    parts = len(qkv)
    seqs, _, rows = segment_rows.shape
    width = qkv[0].shape[1] // 3
    heads = width // HEAD_DIM
    pairs = seqs * heads * rows * rows * parts * parts
    results = pl.pallas_call(
        functools.partial(backward_kernel, heads, parts),
        grid=(seqs,),
        in_specs=[row_spec(rows, 3 * width)] * parts
        + [row_spec(rows, width)] * parts
        + [cube_spec(heads, rows)] * parts
        + [cube_spec(parts * rows, 1), cube_spec(parts, rows)],
        out_specs=[row_spec(rows, 3 * width)] * parts + [cube_spec(1, 3 * width)],
        out_shape=[jax.ShapeDtypeStruct((seqs * rows, 3 * width), LOW)] * parts
        + [jax.ShapeDtypeStruct((seqs, 1, 3 * width), WIDE)],
        cost_estimate=pl.CostEstimate(
            flops=10 * pairs * HEAD_DIM,
            bytes_accessed=16 * seqs * rows * width * parts,
            transcendentals=pairs,
        ),
        compiler_params=pltpu.CompilerParams(vmem_limit_bytes=56 << 20),
        name="attend_backward",
    )(*qkv, *grads, *lses, segment_cols, segment_rows)
    return list(results[:parts]), jnp.sum(results[parts], axis=(0, 1))


together = lax.optimization_barrier


def scatter_plan(bits, parts):
    plan = []
    for part in range(parts):
        order = bits if part % 2 == 0 else bits[::-1]
        held = patterns_of(bits)
        for bit in order:
            plan.append((part, bit, tuple(p for p in held if p & bit)))
            held = [p for p in held if not p & bit]
    return plan


def patterns_of(bits):
    patterns = [0]
    for bit in bits:
        patterns += [p | bit for p in patterns]
    return patterns


def scatter_kernel(bits, parts, side, *refs):
    left_refs, right_ref, refs = refs[:parts], refs[parts], refs[parts + 1 :]
    if side:
        stream_refs, out_ref, term_ref, refs = refs[:parts], refs[parts], refs[parts + 1], refs[parts + 2 :]
        streamed, term_sum, term_low, stream_sems, term_sems = refs[8:]
    else:
        out_ref, refs = refs[0], refs[1:]
    far, arrived, held, passed, core_send, core_recv, ring_send, ring_recv = refs[:8]
    rank = lax.axis_index("dp")
    block, width = out_ref.shape[1:]
    stride = min(512, width)

    def across(bit):
        return rank + bit - 2 * bit * (rank // bit % 2)

    barrier = pltpu.get_barrier_semaphore()
    partners = [1] + list(bits)
    for bit in partners:
        pl.semaphore_signal(
            barrier,
            inc=1,
            device_id={"dp": across(bit)},
            device_id_type=pl.DeviceIdType.MESH,
        )
    pl.semaphore_wait(barrier, len(partners))

    patterns = patterns_of(bits)
    place = {p: k for k, p in enumerate(patterns)}

    def tile_rows(part, pattern):
        owner = rank
        for bit in partners:
            if pattern & bit:
                owner = owner + bit - 2 * bit * (rank // bit % 2)
        return left_refs[part].at[pl.ds(pl.multiple_of(owner * block, block), block)]

    def by_columns(function):
        @pl.loop(0, width // stride)
        def _(step):
            function(pl.ds(pl.multiple_of(step * stride, stride), stride))

    deep = left_refs[0].shape[1]
    half_rows = left_refs[0].shape[0] // 2
    lanes = 256 if deep % 256 == 0 else 128
    turns = 2 * (width // stride)

    def stream_copy(part, turn):
        return pltpu.make_async_copy(
            stream_refs[part].at[
                pl.ds(pl.multiple_of(turn % 2 * half_rows, half_rows), half_rows),
                pl.ds(pl.multiple_of(turn // 2 * stride, stride), stride),
            ],
            streamed.at[turn % 2 * parts + part],
            stream_sems.at[turn % 2 * parts + part],
        )

    def term_copy(column):
        return pltpu.make_async_copy(
            term_low.at[column % 2],
            term_ref.at[:, pl.ds(pl.multiple_of(column * stride, stride), stride)],
            term_sems.at[column % 2],
        )

    def side_work(first_turn, last_turn):
        @pl.loop(first_turn, last_turn)
        def _(turn):
            column = turn // 2
            for part in range(parts):
                stream_copy(part, turn).wait()

            @pl.when(turn + 1 < turns)
            def _():
                for part in range(parts):
                    stream_copy(part, turn + 1).start()

            @pl.when(jnp.logical_and(turn % 2 == 1, column >= 2))
            def _():
                term_copy(column - 2).wait()

            @pl.loop(0, deep // lanes)
            def _(step):
                window = pl.ds(pl.multiple_of(step * lanes, lanes), lanes)
                rows = pl.ds(pl.multiple_of(turn % 2 * half_rows, half_rows), half_rows)
                value = sum(
                    contract(left_refs[part][rows, window], streamed[turn % 2 * parts + part], 0, 0)
                    for part in range(parts)
                )

                @pl.when(turn % 2 == 0)
                def _():
                    term_sum[window] = value

                @pl.when(turn % 2 == 1)
                def _():
                    term_low[column % 2, window] = (term_sum[window] + value).astype(LOW)

            @pl.when(turn % 2 == 1)
            def _():
                term_copy(column).start()

    if side:
        for part in range(parts):
            stream_copy(part, 0).start()

    core_copies = {}
    ring_copies = {}
    slot = 0
    plan = scatter_plan(bits, parts)
    for part, bit, moved in plan:
        for pattern in moved:
            ring_copies[part, bit, pattern] = (
                slot,
                pltpu.make_async_remote_copy(
                    src_ref=held.at[part, place[pattern]],
                    dst_ref=passed.at[slot],
                    send_sem=ring_send.at[slot],
                    recv_sem=ring_recv.at[slot],
                    device_id={"dp": across(bit)},
                    device_id_type=pl.DeviceIdType.MESH,
                ),
            )
            slot += 1

    def far_tile(part, pattern):
        rows = tile_rows(part, pattern | 1)
        index = part * len(patterns) + place[pattern]

        def columns(window):
            far[index, :, window] = jnp.dot(
                rows[...], right_ref[:, window], preferred_element_type=WIDE
            ).astype(LOW)

        by_columns(columns)
        copy = pltpu.make_async_remote_copy(
            src_ref=far.at[index],
            dst_ref=arrived.at[index],
            send_sem=core_send.at[index],
            recv_sem=core_recv.at[index],
            device_id={"dp": across(1)},
            device_id_type=pl.DeviceIdType.MESH,
        )
        copy.start()
        core_copies[part, pattern] = (index, copy)

    def near_tile(part, pattern):
        rows = tile_rows(part, pattern)
        index, copy = core_copies[part, pattern]
        copy.wait_recv()

        def columns(window):
            value = jnp.dot(
                rows[...], right_ref[:, window], preferred_element_type=WIDE
            ) + arrived[index, :, window].astype(WIDE)
            if pattern:
                held[part, place[pattern], :, window] = value.astype(LOW)
            else:
                out_ref[part, :, window] = value

        by_columns(columns)

    def send(part, bit, moved):
        for pattern in moved:
            ring_copies[part, bit, pattern][1].start()

    def take(part, bit, moved):
        for pattern in moved:
            number, copy = ring_copies[part, bit, pattern]
            copy.wait_recv()
            target = pattern - bit

            def columns(window):
                coming = passed[number, :, window].astype(WIDE)
                if target:
                    old = held[part, place[target], :, window].astype(WIDE)
                    held[part, place[target], :, window] = (old + coming).astype(LOW)
                else:
                    out_ref[part, :, window] = out_ref[part, :, window] + coming

            by_columns(columns)

    steps = [[entry for entry in plan if entry[0] == part] for part in range(parts)]
    first = [steps[part][0] for part in range(parts)]
    urgent = [
        (part, pattern)
        for tiles in zip(*[sorted(entry[2], reverse=True) for entry in first])
        for part, pattern in enumerate(tiles)
    ]
    others = [
        (part, pattern)
        for pattern in sorted(patterns, reverse=True)
        for part in range(parts)
        if (part, pattern) not in urgent
    ]
    queue = urgent + others
    ahead = 2 * parts
    for entry in queue[:ahead]:
        far_tile(*entry)
    for number, (part, pattern) in enumerate(queue):
        near_tile(part, pattern)
        if (part, pattern) in urgent:
            ring_copies[part, first[part][1], pattern][1].start()
        if number + ahead < len(queue):
            far_tile(*queue[number + ahead])
    for level in range(len(bits)):
        if side and level < 2:
            cut = [0, turns // 2, turns]
            side_work(cut[level], cut[level + 1])
        for part in range(parts):
            take(*steps[part][level])
            if level + 1 < len(bits):
                send(*steps[part][level + 1])
    if side:
        for column in range(max(0, width // stride - 2), width // stride):
            term_copy(column).wait()
    for _, copy in list(core_copies.values()) + list(ring_copies.values()):
        copy.wait_send()


def product_scatter(lefts, right, collective_id, streams=()):
    parts = len(lefts)
    plane = lax.axis_size("dp")
    bits = [1 << k for k in range(1, plane.bit_length() - 1)]
    rows, depth = lefts[0].shape
    width = right.shape[1]
    block = rows // plane
    tiles = plane // 2
    passes = sum(len(moved) for _, _, moved in scatter_plan(bits, parts))
    sent = parts * tiles * block * width * 2 * 2
    stride = min(512, width)
    side = len(streams) > 0
    vmem, anywhere = (
        pl.BlockSpec(memory_space=pltpu.VMEM),
        pl.BlockSpec(memory_space=pl.ANY),
    )
    side_scratch = [
        pltpu.VMEM((2 * parts, rows // 2, stride), LOW),
        pltpu.VMEM((depth, stride), WIDE),
        pltpu.VMEM((2, depth, stride), LOW),
        pltpu.SemaphoreType.DMA((2 * parts,)),
        pltpu.SemaphoreType.DMA((2,)),
    ]
    result = pl.pallas_call(
        functools.partial(scatter_kernel, bits, parts, side),
        out_shape=[jax.ShapeDtypeStruct((parts, block, width), WIDE)]
        + [jax.ShapeDtypeStruct((depth, width), LOW)] * side,
        in_specs=[vmem] * (parts + 1) + [anywhere] * len(streams),
        out_specs=[vmem] + [anywhere] * side,
        scratch_shapes=[
            pltpu.VMEM((parts * tiles, block, width), LOW),
            pltpu.VMEM((parts * tiles, block, width), LOW),
            pltpu.VMEM((parts, tiles, block, width), LOW),
            pltpu.VMEM((passes, block, width), LOW),
            pltpu.SemaphoreType.DMA((parts * tiles,)),
            pltpu.SemaphoreType.DMA((parts * tiles,)),
            pltpu.SemaphoreType.DMA((passes,)),
            pltpu.SemaphoreType.DMA((passes,)),
        ]
        + side_scratch * side,
        cost_estimate=pl.CostEstimate(
            flops=2 * parts * rows * depth * width * (1 + side),
            bytes_accessed=8 * sent,
            transcendentals=0,
        ),
        compiler_params=pltpu.CompilerParams(
            collective_id=collective_id, has_side_effects=True, vmem_limit_bytes=60 << 20
        ),
        name="product_scatter",
    )(*lefts, right, *streams)
    own = [result[0][b] for b in range(parts)]
    return (own, result[1]) if side else own


ROOT = (2.0 / 3.141592653589793) ** 0.5


def gelu_slope(values_in):
    squared = values_in * values_in
    bend = jnp.tanh(ROOT * values_in * (1.0 + 0.044715 * squared))
    slope = ROOT * (1.0 + 3.0 * 0.044715 * squared)
    return 0.5 * (1.0 + bend) + 0.5 * values_in * (1.0 - bend * bend) * slope


def gather_kernel(bits, parts, mode, *refs):
    backward, plain = mode == "slope", mode == "plain"
    block_refs = refs[:parts]
    weight_ref = refs[parts]
    rest = refs[parts + 1 :]
    if backward:
        wide_refs, rest = rest[:parts], rest[parts:]
        gathered_refs, low_refs, rest = rest[:parts], rest[parts : 2 * parts], rest[2 * parts :]
    elif plain:
        wide_refs = None
        gathered_refs, low_refs, rest = rest[:parts], rest[parts : 2 * parts], rest[2 * parts :]
    else:
        bias_ref, rest = rest[0], rest[1:]
        gathered_refs, wide_refs = rest[:parts], rest[parts : 2 * parts]
        low_refs, rest = rest[2 * parts : 3 * parts], rest[3 * parts :]
    landed, wide_stage, low_stage = rest[:3]
    send_sems, recv_sems, keep_sems, wide_sems, low_sems = rest[3:]
    rank = lax.axis_index("dp")
    block = block_refs[0].shape[0]
    hidden = weight_ref.shape[0]
    stride = min(512, hidden)

    def across(bit):
        return rank + bit - 2 * bit * (rank // bit % 2)

    barrier = pltpu.get_barrier_semaphore()
    partners = [1] + list(bits)
    for bit in partners:
        pl.semaphore_signal(
            barrier,
            inc=1,
            device_id={"dp": across(bit)},
            device_id_type=pl.DeviceIdType.MESH,
        )
    pl.semaphore_wait(barrier, len(partners))

    plane = 1 << len(partners)
    orders = [list(bits) if part % 2 == 0 else list(bits)[::-1] for part in range(parts)]
    near = [patterns_of(order) for order in orders]
    copies = {}

    def slot(part, pattern):
        return part * plane + pattern

    def source(part, pattern):
        return landed.at[slot(part, pattern)] if pattern else block_refs[part]

    def pass_on(part, pattern, bit):
        target = slot(part, pattern | bit)
        copy = pltpu.make_async_remote_copy(
            src_ref=source(part, pattern),
            dst_ref=landed.at[target],
            send_sem=send_sems.at[target],
            recv_sem=recv_sems.at[target],
            device_id={"dp": across(bit)},
            device_id_type=pl.DeviceIdType.MESH,
        )
        copy.start()
        copies[part, pattern | bit] = copy

    def place_of(pattern):
        owner = rank
        for bit in partners:
            if pattern & bit:
                owner = owner + bit - 2 * bit * (rank // bit % 2)
        return pl.ds(pl.multiple_of(owner * block, block), block)

    kept = []

    def keep(part, pattern):
        copy = pltpu.make_async_copy(
            source(part, pattern),
            gathered_refs[part].at[place_of(pattern)],
            keep_sems.at[slot(part, pattern)],
        )
        copy.start()
        kept.append(copy)

    sequence = []
    for turn in range(len(near[0])):
        sequence += [(part, near[part][turn]) for part in range(parts)]
        sequence += [(part, near[part][turn] | 1) for part in range(parts)]
    stored = {}

    def fetch(number):
        part, pattern = sequence[number]
        copy = pltpu.make_async_copy(
            wide_refs[part].at[place_of(pattern)],
            wide_stage.at[number % 2],
            wide_sems.at[number % 2],
        )
        copy.start()
        return copy

    def multiply(number):
        part, pattern = sequence[number]
        turn = number % 2
        rows = source(part, pattern)
        for copy in stored.pop(number - 2, ()):
            copy.wait()
        if backward:
            stored_wide.pop(number).wait()

        @pl.loop(0, hidden // stride)
        def _(step):
            window = pl.ds(pl.multiple_of(step * stride, stride), stride)
            product = contract(rows[...], weight_ref[window], 1, 1)
            if backward:
                value = product * gelu_slope(wide_stage[turn, :, window])
            elif plain:
                value = product
            else:
                value = product + bias_ref[:, window]
                wide_stage[turn, :, window] = value
                value = gelu_tanh(value)
            low_stage[turn, :, window] = value.astype(LOW)

        if backward and number + 2 < len(sequence):
            stored_wide[number + 2] = fetch(number + 2)
        outgoing = [
            pltpu.make_async_copy(
                low_stage.at[turn], low_refs[part].at[place_of(pattern)], low_sems.at[turn]
            )
        ]
        if not backward and not plain:
            outgoing.append(
                pltpu.make_async_copy(
                    wide_stage.at[turn], wide_refs[part].at[place_of(pattern)], wide_sems.at[turn]
                )
            )
        for copy in outgoing:
            copy.start()
        stored[number] = outgoing

    stored_wide = {}
    if backward:
        for number in range(2):
            stored_wide[number] = fetch(number)
    for turn in range(len(bits)):
        for part in range(parts):
            pass_on(part, 0, orders[part][turn])
    for part in range(parts):
        pass_on(part, 0, 1)
        keep(part, 0)

    number = 0
    for turn in range(len(near[0])):
        if turn:
            for part in range(parts):
                pattern = near[part][turn]
                copies[part, pattern].wait_recv()
                highest = max(orders[part].index(bit) for bit in bits if pattern & bit)
                for bit in orders[part][highest + 1 :]:
                    pass_on(part, pattern, bit)
                pass_on(part, pattern, 1)
                keep(part, pattern)
        for part in range(parts):
            multiply(number)
            number += 1
        for part in range(parts):
            pattern = near[part][turn] | 1
            copies[part, pattern].wait_recv()
            keep(part, pattern)
            multiply(number)
            number += 1
    for outgoing in stored.values():
        for copy in outgoing:
            copy.wait()
    for copy in kept:
        copy.wait()
    for copy in copies.values():
        copy.wait_send()


def gather_product(blocks, weight, extra, collective_id):
    mode = "plain" if extra is None else "slope" if isinstance(extra, list) else "bias"
    parts = len(blocks)
    plane = lax.axis_size("dp")
    bits = [1 << k for k in range(1, plane.bit_length() - 1)]
    block, width = blocks[0].shape
    hidden = weight.shape[0]
    rows = plane * block
    vmem, anywhere = (
        pl.BlockSpec(memory_space=pltpu.VMEM),
        pl.BlockSpec(memory_space=pl.ANY),
    )
    gathered = jax.ShapeDtypeStruct((rows, width), LOW)
    wide = jax.ShapeDtypeStruct((rows, hidden), WIDE)
    low = jax.ShapeDtypeStruct((rows, hidden), LOW)
    outs = [gathered] * parts + ([wide] * parts if mode == "bias" else []) + [low] * parts
    extras = {"plain": [], "bias": [extra], "slope": extra}[mode]
    results = pl.pallas_call(
        functools.partial(gather_kernel, bits, parts, mode),
        out_shape=outs,
        in_specs=[vmem] * (parts + 1) + [anywhere if mode == "slope" else vmem] * len(extras),
        out_specs=[anywhere] * len(outs),
        scratch_shapes=[
            pltpu.VMEM((parts * plane, block, width), LOW),
            pltpu.VMEM((2, block, hidden), WIDE),
            pltpu.VMEM((2, block, hidden), LOW),
            pltpu.SemaphoreType.DMA((parts * plane,)),
            pltpu.SemaphoreType.DMA((parts * plane,)),
            pltpu.SemaphoreType.DMA((parts * plane,)),
            pltpu.SemaphoreType.DMA((2,)),
            pltpu.SemaphoreType.DMA((2,)),
        ],
        cost_estimate=pl.CostEstimate(
            flops=2 * parts * rows * hidden * width,
            bytes_accessed=16 * parts * rows * width,
            transcendentals=parts * rows * hidden,
        ),
        compiler_params=pltpu.CompilerParams(
            collective_id=collective_id, has_side_effects=True, vmem_limit_bytes=60 << 20
        ),
        name="gather_product",
    )(*blocks, weight, *extras)
    return [list(results[k : k + parts]) for k in range(0, len(outs), parts)]


def opening_kernel(bits, parts, depth, *refs):
    block_refs, piece_ref = refs[:parts], refs[parts]
    gathered_refs, line_ref = refs[parts + 1 : 2 * parts + 1], refs[2 * parts + 1]
    landed, held_line = refs[2 * parts + 2 : 2 * parts + 4]
    send_sems, recv_sems, keep_sems, line_send, line_recv, line_keep = refs[2 * parts + 4 :]
    rank, level = lax.axis_index("dp"), lax.axis_index("mp")
    block = block_refs[0].shape[0]

    def across(bit):
        return rank + bit - 2 * bit * (rank // bit % 2)

    partners = [1] + list(bits)
    plane = 1 << len(partners)
    barrier = pltpu.get_barrier_semaphore()
    for bit in partners:
        pl.semaphore_signal(
            barrier,
            inc=1,
            device_id={"dp": across(bit)},
            device_id_type=pl.DeviceIdType.MESH,
        )
    for shift in (1, depth - 1):
        pl.semaphore_signal(
            barrier,
            inc=1,
            device_id={"mp": (level + shift) % depth},
            device_id_type=pl.DeviceIdType.MESH,
        )
    pl.semaphore_wait(barrier, len(partners) + 2)

    def line_copy(up, step):
        shard = level - step if up else level + step
        number = step * 2 + (0 if up else 1)
        return pltpu.make_async_remote_copy(
            src_ref=held_line.at[shard] if step else piece_ref,
            dst_ref=held_line.at[shard],
            send_sem=line_send.at[number],
            recv_sem=line_recv.at[number],
            device_id={"mp": (level + (1 if up else depth - 1)) % depth},
            device_id_type=pl.DeviceIdType.MESH,
        )

    def sends(up, step):
        if up:
            return jnp.logical_and(level + 1 < depth, level >= step)
        return jnp.logical_and(level > 0, level + step < depth)

    def receives(up, step):
        return level > step if up else level + step + 1 < depth

    orders = [list(bits) if part % 2 == 0 else list(bits)[::-1] for part in range(parts)]
    near = [patterns_of(order) for order in orders]
    copies = {}

    def place_of(pattern):
        owner = rank
        for bit in partners:
            if pattern & bit:
                owner = owner + bit - 2 * bit * (rank // bit % 2)
        return pl.ds(pl.multiple_of(owner * block, block), block)

    def pass_on(part, pattern, bit):
        target = part * plane + (pattern | bit)
        copy = pltpu.make_async_remote_copy(
            src_ref=landed.at[part * plane + pattern] if pattern else block_refs[part],
            dst_ref=landed.at[target],
            send_sem=send_sems.at[target],
            recv_sem=recv_sems.at[target],
            device_id={"dp": across(bit)},
            device_id_type=pl.DeviceIdType.MESH,
        )
        copy.start()
        copies[part, pattern | bit] = copy

    def line_start(step):
        for up in (True, False):

            @pl.when(sends(up, step))
            def _():
                line_copy(up, step).start()

    line_start(0)
    for turn in range(len(bits)):
        for part in range(parts):
            pass_on(part, 0, orders[part][turn])
    kept = []

    def keep(part, pattern):
        number = part * plane + pattern
        copy = pltpu.make_async_copy(
            landed.at[number] if pattern else block_refs[part],
            gathered_refs[part].at[place_of(pattern)],
            keep_sems.at[number],
        )
        copy.start()
        kept.append(copy)

    def line_keep_copy(up, step):
        shard = level - step if up else level + step
        return pltpu.make_async_copy(
            held_line.at[shard] if step else piece_ref,
            line_ref.at[shard],
            line_keep.at[step * 2 - (0 if up else 1)],
        )

    for part in range(parts):
        pass_on(part, 0, 1)
        keep(part, 0)
    line_keep_copy(True, 0).start()
    for turn in range(1, max(len(near[0]), depth)):
        if turn < len(near[0]):
            for part in range(parts):
                pattern = near[part][turn]
                copies[part, pattern].wait_recv()
                highest = max(orders[part].index(bit) for bit in bits if pattern & bit)
                for bit in orders[part][highest + 1 :]:
                    pass_on(part, pattern, bit)
                pass_on(part, pattern, 1)
                keep(part, pattern)
        if turn < depth:
            for up in (True, False):

                @pl.when(receives(up, turn - 1))
                def _():
                    line_copy(up, turn - 1).wait_recv()
                    line_keep_copy(up, turn).start()

            if turn < depth - 1:
                line_start(turn)
    for part in range(parts):
        for pattern in near[part]:
            copies[part, pattern | 1].wait_recv()
            keep(part, pattern | 1)
    for copy in kept:
        copy.wait()
    for copy in copies.values():
        copy.wait_send()
    line_keep_copy(True, 0).wait()
    for step in range(depth - 1):
        for up in (True, False):

            @pl.when(receives(up, step))
            def _():
                line_keep_copy(up, step + 1).wait()

            @pl.when(sends(up, step))
            def _():
                line_copy(up, step).wait_send()


def opening_gather(blocks, piece, collective_id):
    parts = len(blocks)
    plane, depth = lax.axis_size("dp"), lax.axis_size("mp")
    bits = [1 << k for k in range(1, plane.bit_length() - 1)]
    block, width = blocks[0].shape
    anywhere = pl.BlockSpec(memory_space=pl.ANY)
    results = pl.pallas_call(
        functools.partial(opening_kernel, bits, parts, depth),
        out_shape=[jax.ShapeDtypeStruct((plane * block, width), LOW)] * parts
        + [jax.ShapeDtypeStruct((depth,) + piece.shape, LOW)],
        in_specs=[pl.BlockSpec(memory_space=pltpu.VMEM)] * (parts + 1),
        out_specs=[anywhere] * (parts + 1),
        scratch_shapes=[
            pltpu.VMEM((parts * plane, block, width), LOW),
            pltpu.VMEM((depth,) + piece.shape, LOW),
            pltpu.SemaphoreType.DMA((parts * plane,)),
            pltpu.SemaphoreType.DMA((parts * plane,)),
            pltpu.SemaphoreType.DMA((parts * plane,)),
            pltpu.SemaphoreType.DMA((2 * (depth - 1),)),
            pltpu.SemaphoreType.DMA((2 * (depth - 1),)),
            pltpu.SemaphoreType.DMA((2 * depth - 1,)),
        ],
        cost_estimate=pl.CostEstimate(
            flops=0, bytes_accessed=16 * parts * plane * block * width, transcendentals=0
        ),
        compiler_params=pltpu.CompilerParams(
            collective_id=collective_id, has_side_effects=True, vmem_limit_bytes=60 << 20
        ),
        name="opening_gather",
    )(*blocks, piece)
    return list(results[:parts]), results[parts]


def sum_over(axes, vector):
    for axis in axes:
        size = lax.axis_size(axis)
        step = 1
        while step < size:
            vector = vector + lax.ppermute(vector, axis, [(k, k ^ step) for k in range(size)])
            step *= 2
    return vector


def body(
    inputs,
    segment_ids,
    cotangent,
    query_weight,
    key_weight,
    value_weight,
    out_weight,
    up_weight,
    down_weight,
    query_bias,
    value_bias,
    out_bias,
    up_bias,
    down_bias,
    first_gain,
    first_shift,
    second_gain,
    second_shift,
):
    plane, depth = lax.axis_size("dp"), lax.axis_size("mp")
    rank, level = lax.axis_index("dp"), lax.axis_index("mp")
    parts, block, width = inputs.shape
    length = block * depth
    group = depth // parts
    seqs = plane // group
    rows = group * block
    hidden = up_bias.shape[0] // plane
    heads_in_block = query_weight.shape[1] // HEAD_DIM
    sharers = plane // heads_in_block
    heads = depth // sharers
    parity = level % parts

    def route(turn, back):
        pairs = []
        for i in range(plane):
            for j in range(depth):
                e = (j + turn) % parts
                source = i * depth + j
                target = (i - i % group + j // parts) * depth + parts * (i % group) + e
                pairs.append((target, source) if back else (source, target))
        return pairs

    def pick(options, index):
        return lax.dynamic_index_in_dim(jnp.stack(options), index % parts, 0, keepdims=False)

    def enter(array):
        arrived = [
            lax.ppermute(
                lax.dynamic_index_in_dim(array, (level + turn) % parts, 0, keepdims=False),
                ("dp", "mp"),
                route(turn, False),
            )
            for turn in range(parts)
        ]
        return [pick(arrived, parity - b + parts) for b in range(parts)]

    def leave_picks(blocks):
        return [pick(blocks, parity - turn + parts) for turn in range(parts)]

    def leave_sent(picks):
        return [
            lax.ppermute(picks[turn], ("dp", "mp"), route(turn, True)) for turn in range(parts)
        ]

    def leave_placed(arrived):
        return jnp.stack([pick(arrived, e - parity + parts) for e in range(parts)])

    def swap(array, bit):
        return lax.ppermute(array, "dp", [(k, k ^ bit) for k in range(plane)])

    bits = [1 << k for k in range(plane.bit_length() - 1)]

    sharing = [list(range(k, k + sharers)) for k in range(0, plane, sharers)]

    def share_out(array):
        if sharers == 1:
            return array
        return lax.all_to_all(
            array, "dp", split_axis=0, concat_axis=2, axis_index_groups=sharing, tiled=True
        )

    def share_back(array):
        if sharers == 1:
            return array
        return lax.all_to_all(
            array, "dp", split_axis=2, concat_axis=0, axis_index_groups=sharing, tiled=True
        )

    tokens = enter(inputs)
    attention_shards = jnp.stack([query_weight.T, key_weight.T, value_weight.T, out_weight])
    attention_shards = attention_shards.reshape(4, plane, -1, width // plane)
    attention_pieces = lax.all_to_all(
        attention_shards.transpose(1, 0, 2, 3).reshape(-1, width // plane),
        "dp",
        split_axis=0,
        concat_axis=1,
        tiled=True,
    )
    segments = segment_ids
    for bit in bits:
        other = swap(segments, bit)
        upper = rank // bit % 2 == 1
        segments = jnp.concatenate(
            [jnp.where(upper, other, segments), jnp.where(upper, segments, other)]
        )
    segments = lax.dynamic_index_in_dim(
        segments.reshape(seqs, depth, length), level, 1, keepdims=False
    )
    segments = segments.reshape(seqs, group, parts, block).transpose(0, 2, 1, 3)
    segment_rows = segments.reshape(seqs, parts, rows)
    segment_cols = segments.reshape(seqs, parts * rows, 1)
    tokens, segment_rows, segment_cols = together((tokens, segment_rows, segment_cols))
    forward_shards, attention_pieces = together(((up_weight.T, down_weight), attention_pieces))
    forward_pieces = lax.all_to_all(
        jnp.concatenate(
            [shard.reshape(plane, -1, width // plane) for shard in forward_shards], axis=1
        ).reshape(-1, width // plane),
        "dp",
        split_axis=0,
        concat_axis=1,
        tiled=True,
    )
    gathered_inputs, attention_line = opening_gather(tokens, attention_pieces, 7)
    attention_line, forward_pieces = together((attention_line, forward_pieces))
    up_piece, down_piece = jnp.split(forward_pieces, 2, axis=0)
    attention_full = share_out(attention_line.reshape(depth, 4, -1, width))
    attention_full = attention_full.transpose(1, 0, 2, 3).reshape(4, heads * HEAD_DIM, width)
    full_qkv = attention_full[:3].reshape(3 * heads * HEAD_DIM, width)
    full_out = attention_full[3]

    def own_heads(bias):
        table = bias.reshape(depth, heads_in_block, HEAD_DIM)
        return lax.dynamic_slice(
            table, (rank % sharers * heads, rank // sharers, 0), (heads, 1, HEAD_DIM)
        ).reshape(-1)

    qkv_bias = jnp.concatenate(
        [own_heads(query_bias), jnp.zeros((heads * HEAD_DIM,), WIDE), own_heads(value_bias)]
    )
    own_up = lax.dynamic_slice(
        up_bias.reshape(depth, plane, -1), (0, rank, 0), (depth, 1, hidden // depth)
    ).reshape(-1)

    every = range(parts)
    qkv = [
        (contract(gathered_inputs[b], full_qkv, 1, 1) + qkv_bias).astype(LOW) for b in every
    ]
    full_up = lax.all_gather(up_piece, "mp", axis=0, tiled=True)
    full_down = lax.all_gather(down_piece, "mp", axis=0, tiled=True)
    attended, lses = [], []
    for b in every:
        mixed, lse = attend_forward(b, qkv, segment_cols, segment_rows)
        attended.append(mixed)
        lses.append(lse)
    attn_sums = product_scatter(attended, full_out, 1)
    first = [
        norm_forward(tokens[b].astype(WIDE) + attn_sums[b] + out_bias, first_gain, first_shift)
        for b in every
    ]
    first_low = [first[b][0].astype(LOW) for b in every]
    first_low, full_up, full_down, cotangent = together(
        (first_low, full_up, full_down, cotangent)
    )
    tangents = enter(cotangent)
    gathered_first, up_proj, hiddens = gather_product(
        first_low, full_up, own_up.reshape(1, -1), 4
    )
    hiddens, tangents = together((hiddens, tangents))
    tangents = [array.astype(WIDE) for array in tangents]
    ffn_sums = product_scatter(hiddens, full_down, 2)
    second = [
        norm_forward(first[b][0] + ffn_sums[b] + down_bias, second_gain, second_shift)
        for b in every
    ]
    outputs = leave_placed(
        leave_sent(leave_picks([second[b][0].astype(LOW) for b in every]))
    )

    def share_attention(term):
        return share_back(term.reshape(-1, heads, HEAD_DIM, width).transpose(1, 0, 2, 3))

    def reduce_attention(term):
        return lax.psum_scatter(share_attention(term), "mp", scatter_dimension=0, tiled=True)[0]

    def reduce_forward(term):
        return lax.psum_scatter(term, "mp", scatter_dimension=0, tiled=True)

    def owner_exchange(term):
        return lax.all_to_all(
            term.reshape(-1, width), "dp", split_axis=1, concat_axis=0, tiled=True
        )

    def low_sum(terms):
        return sum(terms).astype(LOW)

    def total(arrays):
        return sum(jnp.sum(array.astype(WIDE), axis=0) for array in arrays)

    grad_second_gain = total([tangents[b] * second[b][1] for b in every])
    grad_second_shift = total(tangents)
    grad_two = [
        norm_backward(tangents[b], second[b][1], second[b][2], second_gain) for b in every
    ]
    grad_ffn = [array.astype(LOW) for array in grad_two]
    grad_down_bias = total(grad_ffn)
    gathered_ffn, grad_upper = gather_product(grad_ffn, full_down, up_proj, 5)
    gathered_ffn, grad_upper, outputs = together((gathered_ffn, grad_upper, outputs))
    grad_up_bias = total(grad_upper)
    back_sums, term_up = product_scatter(grad_upper, full_up, 8, gathered_first)
    term_down = low_sum(contract(hiddens[b], gathered_ffn[b], 0, 0) for b in every)
    grad_first = [grad_two[b] + back_sums[b] for b in every]
    grad_first_gain = total([grad_first[b] * first[b][1] for b in every])
    grad_first_shift = total(grad_first)
    grad_resid = [
        norm_backward(grad_first[b], first[b][1], first[b][2], first_gain) for b in every
    ]
    grad_branch = [array.astype(LOW) for array in grad_resid]
    reduced_down = reduce_forward(term_down)
    grad_branch, reduced_down = together((grad_branch, reduced_down))
    grad_out_bias = total(grad_branch)
    gathered_branch, grad_mixed = gather_product(grad_branch, full_out, None, 6)
    spread_up = lax.dynamic_update_slice(
        jnp.zeros((depth, plane, hidden // depth), WIDE),
        grad_up_bias.reshape(depth, 1, -1),
        (0, rank, 0),
    ).reshape(-1)
    owned_down = owner_exchange(reduced_down)
    reduced_up = reduce_forward(term_up)
    grad_mixed = [
        array.reshape(seqs * rows, heads * HEAD_DIM)
        for array in grad_mixed
    ]
    grad_qkv, grad_qkv_bias = attend_backward(qkv, grad_mixed, lses, segment_cols, segment_rows)

    def spread_heads(piece):
        table = jnp.zeros((depth, heads_in_block, HEAD_DIM), WIDE)
        return lax.dynamic_update_slice(
            table,
            piece.reshape(heads, 1, HEAD_DIM),
            (rank % sharers * heads, rank // sharers, 0),
        ).reshape(-1)

    spread = heads * HEAD_DIM
    vectors = jnp.concatenate(
        [
            spread_heads(grad_qkv_bias[:spread]),
            spread_heads(grad_qkv_bias[2 * spread :]),
            grad_out_bias,
            grad_down_bias,
            grad_first_gain,
            grad_first_shift,
            grad_second_gain,
            grad_second_shift,
            spread_up,
        ]
    )
    vectors = sum_over(("mp",), vectors.reshape(-1, HEAD_DIM))
    reduced_out = reduce_attention(
        low_sum(contract(attended[b], gathered_branch[b], 0, 0) for b in every)
    )
    term_qkv = low_sum(contract(grad_qkv[b], gathered_inputs[b], 0, 0) for b in every)
    term_qkv, reduced_up = together((term_qkv, reduced_up))
    shared_qkv = share_attention(term_qkv)
    owned_up = owner_exchange(reduced_up)
    grad_qkv, shared_qkv, vectors = together((grad_qkv, shared_qkv, vectors))
    input_sums = product_scatter(grad_qkv, full_qkv, 3)
    reduced_qkv = lax.psum_scatter(shared_qkv, "mp", scatter_dimension=0, tiled=True)[0]
    grad_low = [(grad_resid[b] + input_sums[b]).astype(LOW) for b in every]
    leaving = leave_sent(leave_picks(grad_low))
    vectors = sum_over(("dp",), vectors).reshape(-1)
    grad_inputs = leave_placed(leaving).astype(WIDE)

    owned_out = owner_exchange(reduced_out)
    owned_qkv = owner_exchange(reduced_qkv)
    owned_qkv = owned_qkv.reshape(plane, 3, -1, width // plane).transpose(1, 0, 2, 3)
    owned_qkv = owned_qkv.reshape(3, -1, width // plane)

    narrow = vectors[: 8 * width].reshape(8, width)
    return (
        outputs,
        grad_inputs,
        owned_qkv[0].T.astype(WIDE),
        owned_qkv[1].T.astype(WIDE),
        owned_qkv[2].T.astype(WIDE),
        owned_out.astype(WIDE),
        owned_up.T.astype(WIDE),
        owned_down.astype(WIDE),
        narrow[0],
        narrow[1],
        narrow[2],
        vectors[8 * width :],
        narrow[3],
        narrow[4],
        narrow[5],
        narrow[6],
        narrow[7],
    )


def solution(mesh):
    tokens = P("dp", "mp", None)
    by_rows, by_columns, whole = P("dp", "mp"), P("mp", "dp"), P()
    in_specs = (
        (tokens, P("dp", None), tokens)
        + (by_rows,) * 3
        + (by_columns, by_rows, by_columns)
        + (whole,) * 9
    )
    out_specs = (
        (tokens, tokens) + (by_rows,) * 3 + (by_columns, by_rows, by_columns) + (whole,) * 9
    )
    return jax.shard_map(body, mesh=mesh, in_specs=in_specs, out_specs=out_specs, check_vma=False)
```

```python
import functools

import jax
import jax.numpy as jnp
from jax import lax
from jax.experimental import pallas as pl
from jax.experimental.pallas import tpu as pltpu
from jax.sharding import PartitionSpec as P


HEAD_DIM = 128
SCALING = HEAD_DIM ** (-0.5)
EPSILON = 1e-12
MASKED = -1e30
LOW = jnp.bfloat16
WIDE = jnp.float32


def contract(left, right, left_dim, right_dim):
    return lax.dot_general(
        left, right, (((left_dim,), (right_dim,)), ((), ())), preferred_element_type=WIDE
    )


def norm_forward(resid, scale_vec, shift_vec):
    average = jnp.mean(resid, axis=-1, keepdims=True)
    centered = resid - average
    variance = jnp.mean(centered * centered, axis=-1, keepdims=True)
    inv_std = lax.rsqrt(variance + EPSILON)
    normed = centered * inv_std
    return normed * scale_vec + shift_vec, normed, inv_std


def norm_backward(upstream, normed, inv_std, scale_vec):
    scaled = upstream * scale_vec
    first_mean = jnp.mean(scaled, axis=-1, keepdims=True)
    second_mean = jnp.mean(scaled * normed, axis=-1, keepdims=True)
    return inv_std * (scaled - first_mean - normed * second_mean)


def gelu_tanh(values_in):
    return jax.nn.gelu(values_in, approximate=True)


def head_rows(refs, column):
    return jnp.concatenate([ref[:, column : column + HEAD_DIM] for ref in refs], axis=0)


def forward_kernel(heads, parts, which, *refs):
    qkv_refs = refs[:parts]
    keys_segment, query_segments, out_ref, lse_ref = refs[parts:]
    segment_col = keys_segment[0]
    segment_row = query_segments[0, which : which + 1]
    allowed = segment_col == segment_row
    for head in range(heads):
        queries = qkv_refs[which][:, head * HEAD_DIM : (head + 1) * HEAD_DIM]
        keys_all = head_rows(qkv_refs, (heads + head) * HEAD_DIM)
        values_all = head_rows(qkv_refs, (2 * heads + head) * HEAD_DIM)
        logits = jnp.where(allowed, contract(keys_all, queries, 1, 1) * SCALING, MASKED)
        top = jnp.max(logits, axis=0, keepdims=True)
        expo = jnp.exp(logits - top)
        total = jnp.sum(expo, axis=0, keepdims=True)
        probs_low = (expo * (1.0 / total)).astype(LOW)
        mixed = contract(values_all, probs_low, 0, 0)
        out_ref[:, head * HEAD_DIM : (head + 1) * HEAD_DIM] = mixed.T.astype(LOW)
        lse_ref[0, head : head + 1] = top + jnp.log(total)


def backward_kernel(heads, parts, *refs):
    qkv_refs = refs[:parts]
    grad_refs = refs[parts : 2 * parts]
    lse_refs = refs[2 * parts : 3 * parts]
    keys_segment, query_segments = refs[3 * parts : 3 * parts + 2]
    out_refs = refs[3 * parts + 2 : 4 * parts + 2]
    bias_ref = refs[4 * parts + 2]
    rows = qkv_refs[0].shape[0]
    segment_col = keys_segment[0]
    bias_ref[...] = jnp.zeros_like(bias_ref)
    for head in range(heads):
        base = head * HEAD_DIM
        keys_all = head_rows(qkv_refs, heads * HEAD_DIM + base)
        values_all = head_rows(qkv_refs, 2 * heads * HEAD_DIM + base)
        grad_keys = 0.0
        grad_values = 0.0
        query_bias = 0.0
        for which in range(parts):
            queries = qkv_refs[which][:, base : base + HEAD_DIM]
            grad_mixed = grad_refs[which][:, base : base + HEAD_DIM]
            allowed = segment_col == query_segments[0, which : which + 1]
            logits = contract(keys_all, queries, 1, 1) * SCALING
            probs = jnp.where(allowed, jnp.exp(logits - lse_refs[which][0, head : head + 1]), 0.0)
            grad_probs = contract(values_all, grad_mixed, 1, 1)
            inner = jnp.sum(probs * grad_probs, axis=0, keepdims=True)
            grad_logits = (probs * (grad_probs - inner)).astype(LOW)
            probs_low = probs.astype(LOW)
            grad_values = grad_values + jnp.dot(
                probs_low, grad_mixed, preferred_element_type=WIDE
            )
            grad_keys = grad_keys + jnp.dot(grad_logits, queries, preferred_element_type=WIDE)
            grad_queries = (contract(keys_all, grad_logits, 0, 0) * SCALING).T.astype(LOW)
            query_bias = query_bias + jnp.sum(grad_queries.astype(WIDE), axis=0, keepdims=True)
            out_refs[which][:, base : base + HEAD_DIM] = grad_queries
        grad_keys = (grad_keys * SCALING).astype(LOW)
        grad_values = grad_values.astype(LOW)
        bias_ref[0, :, base : base + HEAD_DIM] = query_bias
        start = 2 * heads * HEAD_DIM + base
        bias_ref[0, :, start : start + HEAD_DIM] = jnp.sum(
            grad_values.astype(WIDE), axis=0, keepdims=True
        )
        for which in range(parts):
            piece = slice(which * rows, (which + 1) * rows)
            start = heads * HEAD_DIM + base
            out_refs[which][:, start : start + HEAD_DIM] = grad_keys[piece]
            start = 2 * heads * HEAD_DIM + base
            out_refs[which][:, start : start + HEAD_DIM] = grad_values[piece]


def row_spec(rows, width):
    return pl.BlockSpec((rows, width), lambda s: (s, 0))


def cube_spec(*dims):
    return pl.BlockSpec((1,) + dims, lambda s: (s, 0, 0))


def attend_forward(which, qkv, segment_cols, segment_rows):
    parts = len(qkv)
    seqs, _, rows = segment_rows.shape
    width = qkv[0].shape[1] // 3
    heads = width // HEAD_DIM
    pairs = seqs * heads * rows * rows * parts
    return pl.pallas_call(
        functools.partial(forward_kernel, heads, parts, which),
        grid=(seqs,),
        in_specs=[row_spec(rows, 3 * width)] * parts
        + [cube_spec(parts * rows, 1), cube_spec(parts, rows)],
        out_specs=[row_spec(rows, width), cube_spec(heads, rows)],
        out_shape=[
            jax.ShapeDtypeStruct((seqs * rows, width), LOW),
            jax.ShapeDtypeStruct((seqs, heads, rows), WIDE),
        ],
        cost_estimate=pl.CostEstimate(
            flops=4 * pairs * HEAD_DIM,
            bytes_accessed=8 * seqs * rows * width * parts,
            transcendentals=pairs,
        ),
        compiler_params=pltpu.CompilerParams(vmem_limit_bytes=56 << 20),
        name="attend_forward",
    )(*qkv, segment_cols, segment_rows)


def attend_backward(qkv, grads, lses, segment_cols, segment_rows):
    parts = len(qkv)
    seqs, _, rows = segment_rows.shape
    width = qkv[0].shape[1] // 3
    heads = width // HEAD_DIM
    pairs = seqs * heads * rows * rows * parts * parts
    results = pl.pallas_call(
        functools.partial(backward_kernel, heads, parts),
        grid=(seqs,),
        in_specs=[row_spec(rows, 3 * width)] * parts
        + [row_spec(rows, width)] * parts
        + [cube_spec(heads, rows)] * parts
        + [cube_spec(parts * rows, 1), cube_spec(parts, rows)],
        out_specs=[row_spec(rows, 3 * width)] * parts + [cube_spec(1, 3 * width)],
        out_shape=[jax.ShapeDtypeStruct((seqs * rows, 3 * width), LOW)] * parts
        + [jax.ShapeDtypeStruct((seqs, 1, 3 * width), WIDE)],
        cost_estimate=pl.CostEstimate(
            flops=10 * pairs * HEAD_DIM,
            bytes_accessed=16 * seqs * rows * width * parts,
            transcendentals=pairs,
        ),
        compiler_params=pltpu.CompilerParams(vmem_limit_bytes=56 << 20),
        name="attend_backward",
    )(*qkv, *grads, *lses, segment_cols, segment_rows)
    return list(results[:parts]), jnp.sum(results[parts], axis=(0, 1))


together = lax.optimization_barrier


def scatter_plan(bits, parts):
    plan = []
    for part in range(parts):
        order = bits if part % 2 == 0 else bits[::-1]
        held = patterns_of(bits)
        for bit in order:
            plan.append((part, bit, tuple(p for p in held if p & bit)))
            held = [p for p in held if not p & bit]
    return plan


def patterns_of(bits):
    patterns = [0]
    for bit in bits:
        patterns += [p | bit for p in patterns]
    return patterns


def scatter_kernel(bits, parts, side, *refs):
    left_refs, right_ref, refs = refs[:parts], refs[parts], refs[parts + 1 :]
    if side:
        stream_refs, out_ref, term_ref, refs = refs[:parts], refs[parts], refs[parts + 1], refs[parts + 2 :]
        streamed, term_sum, term_low, stream_sems, term_sems = refs[8:]
    else:
        out_ref, refs = refs[0], refs[1:]
    far, arrived, held, passed, core_send, core_recv, ring_send, ring_recv = refs[:8]
    rank = lax.axis_index("dp")
    block, width = out_ref.shape[1:]
    stride = min(512, width)

    def across(bit):
        return rank + bit - 2 * bit * (rank // bit % 2)

    barrier = pltpu.get_barrier_semaphore()
    partners = [1] + list(bits)
    for bit in partners:
        pl.semaphore_signal(
            barrier,
            inc=1,
            device_id={"dp": across(bit)},
            device_id_type=pl.DeviceIdType.MESH,
        )
    pl.semaphore_wait(barrier, len(partners))

    patterns = patterns_of(bits)
    place = {p: k for k, p in enumerate(patterns)}

    def tile_rows(part, pattern):
        owner = rank
        for bit in partners:
            if pattern & bit:
                owner = owner + bit - 2 * bit * (rank // bit % 2)
        return left_refs[part].at[pl.ds(pl.multiple_of(owner * block, block), block)]

    def by_columns(function):
        @pl.loop(0, width // stride)
        def _(step):
            function(pl.ds(pl.multiple_of(step * stride, stride), stride))

    deep = left_refs[0].shape[1]
    half_rows = left_refs[0].shape[0] // 2
    lanes = 256 if deep % 256 == 0 else 128
    turns = 2 * (width // stride)

    def stream_copy(part, turn):
        return pltpu.make_async_copy(
            stream_refs[part].at[
                pl.ds(pl.multiple_of(turn % 2 * half_rows, half_rows), half_rows),
                pl.ds(pl.multiple_of(turn // 2 * stride, stride), stride),
            ],
            streamed.at[turn % 2 * parts + part],
            stream_sems.at[turn % 2 * parts + part],
        )

    def term_copy(column):
        return pltpu.make_async_copy(
            term_low.at[column % 2],
            term_ref.at[:, pl.ds(pl.multiple_of(column * stride, stride), stride)],
            term_sems.at[column % 2],
        )

    def side_work(first_turn, last_turn):
        @pl.loop(first_turn, last_turn)
        def _(turn):
            column = turn // 2
            for part in range(parts):
                stream_copy(part, turn).wait()

            @pl.when(turn + 1 < turns)
            def _():
                for part in range(parts):
                    stream_copy(part, turn + 1).start()

            @pl.when(jnp.logical_and(turn % 2 == 1, column >= 2))
            def _():
                term_copy(column - 2).wait()

            @pl.loop(0, deep // lanes)
            def _(step):
                window = pl.ds(pl.multiple_of(step * lanes, lanes), lanes)
                rows = pl.ds(pl.multiple_of(turn % 2 * half_rows, half_rows), half_rows)
                value = sum(
                    contract(left_refs[part][rows, window], streamed[turn % 2 * parts + part], 0, 0)
                    for part in range(parts)
                )

                @pl.when(turn % 2 == 0)
                def _():
                    term_sum[window] = value

                @pl.when(turn % 2 == 1)
                def _():
                    term_low[column % 2, window] = (term_sum[window] + value).astype(LOW)

            @pl.when(turn % 2 == 1)
            def _():
                term_copy(column).start()

    if side:
        for part in range(parts):
            stream_copy(part, 0).start()

    core_copies = {}
    ring_copies = {}
    slot = 0
    plan = scatter_plan(bits, parts)
    for part, bit, moved in plan:
        for pattern in moved:
            ring_copies[part, bit, pattern] = (
                slot,
                pltpu.make_async_remote_copy(
                    src_ref=held.at[part, place[pattern]],
                    dst_ref=passed.at[slot],
                    send_sem=ring_send.at[slot],
                    recv_sem=ring_recv.at[slot],
                    device_id={"dp": across(bit)},
                    device_id_type=pl.DeviceIdType.MESH,
                ),
            )
            slot += 1

    def far_tile(part, pattern):
        rows = tile_rows(part, pattern | 1)
        index = part * len(patterns) + place[pattern]

        def columns(window):
            far[index, :, window] = jnp.dot(
                rows[...], right_ref[:, window], preferred_element_type=WIDE
            ).astype(LOW)

        by_columns(columns)
        copy = pltpu.make_async_remote_copy(
            src_ref=far.at[index],
            dst_ref=arrived.at[index],
            send_sem=core_send.at[index],
            recv_sem=core_recv.at[index],
            device_id={"dp": across(1)},
            device_id_type=pl.DeviceIdType.MESH,
        )
        copy.start()
        core_copies[part, pattern] = (index, copy)

    def near_tile(part, pattern):
        rows = tile_rows(part, pattern)
        index, copy = core_copies[part, pattern]
        copy.wait_recv()

        def columns(window):
            value = jnp.dot(
                rows[...], right_ref[:, window], preferred_element_type=WIDE
            ) + arrived[index, :, window].astype(WIDE)
            if pattern:
                held[part, place[pattern], :, window] = value.astype(LOW)
            else:
                out_ref[part, :, window] = value

        by_columns(columns)

    def send(part, bit, moved):
        for pattern in moved:
            ring_copies[part, bit, pattern][1].start()

    def take(part, bit, moved):
        for pattern in moved:
            number, copy = ring_copies[part, bit, pattern]
            copy.wait_recv()
            target = pattern - bit

            def columns(window):
                coming = passed[number, :, window].astype(WIDE)
                if target:
                    old = held[part, place[target], :, window].astype(WIDE)
                    held[part, place[target], :, window] = (old + coming).astype(LOW)
                else:
                    out_ref[part, :, window] = out_ref[part, :, window] + coming

            by_columns(columns)

    steps = [[entry for entry in plan if entry[0] == part] for part in range(parts)]
    first = [steps[part][0] for part in range(parts)]
    urgent = [
        (part, pattern)
        for tiles in zip(*[sorted(entry[2], reverse=True) for entry in first])
        for part, pattern in enumerate(tiles)
    ]
    others = [
        (part, pattern)
        for pattern in sorted(patterns, reverse=True)
        for part in range(parts)
        if (part, pattern) not in urgent
    ]
    queue = urgent + others
    ahead = parts
    for entry in queue[:ahead]:
        far_tile(*entry)
    for number, (part, pattern) in enumerate(queue):
        near_tile(part, pattern)
        if (part, pattern) in urgent:
            ring_copies[part, first[part][1], pattern][1].start()
        if number + ahead < len(queue):
            far_tile(*queue[number + ahead])
    for level in range(len(bits)):
        if side and level < 2:
            cut = [0, turns // 2, turns]
            side_work(cut[level], cut[level + 1])
        for part in range(parts):
            take(*steps[part][level])
            if level + 1 < len(bits):
                send(*steps[part][level + 1])
    if side:
        for column in range(max(0, width // stride - 2), width // stride):
            term_copy(column).wait()
    for _, copy in list(core_copies.values()) + list(ring_copies.values()):
        copy.wait_send()


def product_scatter(lefts, right, collective_id, streams=()):
    parts = len(lefts)
    plane = lax.axis_size("dp")
    bits = [1 << k for k in range(1, plane.bit_length() - 1)]
    rows, depth = lefts[0].shape
    width = right.shape[1]
    block = rows // plane
    tiles = plane // 2
    passes = sum(len(moved) for _, _, moved in scatter_plan(bits, parts))
    sent = parts * tiles * block * width * 2 * 2
    stride = min(512, width)
    side = len(streams) > 0
    vmem, anywhere = (
        pl.BlockSpec(memory_space=pltpu.VMEM),
        pl.BlockSpec(memory_space=pl.ANY),
    )
    side_scratch = [
        pltpu.VMEM((2 * parts, rows // 2, stride), LOW),
        pltpu.VMEM((depth, stride), WIDE),
        pltpu.VMEM((2, depth, stride), LOW),
        pltpu.SemaphoreType.DMA((2 * parts,)),
        pltpu.SemaphoreType.DMA((2,)),
    ]
    result = pl.pallas_call(
        functools.partial(scatter_kernel, bits, parts, side),
        out_shape=[jax.ShapeDtypeStruct((parts, block, width), WIDE)]
        + [jax.ShapeDtypeStruct((depth, width), LOW)] * side,
        in_specs=[vmem] * (parts + 1) + [anywhere] * len(streams),
        out_specs=[vmem] + [anywhere] * side,
        scratch_shapes=[
            pltpu.VMEM((parts * tiles, block, width), LOW),
            pltpu.VMEM((parts * tiles, block, width), LOW),
            pltpu.VMEM((parts, tiles, block, width), LOW),
            pltpu.VMEM((passes, block, width), LOW),
            pltpu.SemaphoreType.DMA((parts * tiles,)),
            pltpu.SemaphoreType.DMA((parts * tiles,)),
            pltpu.SemaphoreType.DMA((passes,)),
            pltpu.SemaphoreType.DMA((passes,)),
        ]
        + side_scratch * side,
        cost_estimate=pl.CostEstimate(
            flops=2 * parts * rows * depth * width * (1 + side),
            bytes_accessed=8 * sent,
            transcendentals=0,
        ),
        compiler_params=pltpu.CompilerParams(
            collective_id=collective_id, has_side_effects=True, vmem_limit_bytes=60 << 20
        ),
        name="product_scatter",
    )(*lefts, right, *streams)
    own = [result[0][b] for b in range(parts)]
    return (own, result[1]) if side else own


ROOT = (2.0 / 3.141592653589793) ** 0.5


def gelu_slope(values_in):
    squared = values_in * values_in
    bend = jnp.tanh(ROOT * values_in * (1.0 + 0.044715 * squared))
    slope = ROOT * (1.0 + 3.0 * 0.044715 * squared)
    return 0.5 * (1.0 + bend) + 0.5 * values_in * (1.0 - bend * bend) * slope


def gather_kernel(bits, parts, mode, *refs):
    backward, plain = mode == "slope", mode == "plain"
    block_refs = refs[:parts]
    weight_ref = refs[parts]
    rest = refs[parts + 1 :]
    if backward:
        wide_refs, rest = rest[:parts], rest[parts:]
        gathered_refs, low_refs, rest = rest[:parts], rest[parts : 2 * parts], rest[2 * parts :]
    elif plain:
        wide_refs = None
        gathered_refs, low_refs, rest = rest[:parts], rest[parts : 2 * parts], rest[2 * parts :]
    else:
        bias_ref, rest = rest[0], rest[1:]
        gathered_refs, wide_refs = rest[:parts], rest[parts : 2 * parts]
        low_refs, rest = rest[2 * parts : 3 * parts], rest[3 * parts :]
    landed, wide_stage, low_stage = rest[:3]
    send_sems, recv_sems, keep_sems, wide_sems, low_sems = rest[3:]
    rank = lax.axis_index("dp")
    block = block_refs[0].shape[0]
    hidden = weight_ref.shape[0]
    stride = min(512, hidden)

    def across(bit):
        return rank + bit - 2 * bit * (rank // bit % 2)

    barrier = pltpu.get_barrier_semaphore()
    partners = [1] + list(bits)
    for bit in partners:
        pl.semaphore_signal(
            barrier,
            inc=1,
            device_id={"dp": across(bit)},
            device_id_type=pl.DeviceIdType.MESH,
        )
    pl.semaphore_wait(barrier, len(partners))

    plane = 1 << len(partners)
    orders = [list(bits) if part % 2 == 0 else list(bits)[::-1] for part in range(parts)]
    near = [patterns_of(order) for order in orders]
    copies = {}

    def slot(part, pattern):
        return part * plane + pattern

    def source(part, pattern):
        return landed.at[slot(part, pattern)] if pattern else block_refs[part]

    def pass_on(part, pattern, bit):
        target = slot(part, pattern | bit)
        copy = pltpu.make_async_remote_copy(
            src_ref=source(part, pattern),
            dst_ref=landed.at[target],
            send_sem=send_sems.at[target],
            recv_sem=recv_sems.at[target],
            device_id={"dp": across(bit)},
            device_id_type=pl.DeviceIdType.MESH,
        )
        copy.start()
        copies[part, pattern | bit] = copy

    def place_of(pattern):
        owner = rank
        for bit in partners:
            if pattern & bit:
                owner = owner + bit - 2 * bit * (rank // bit % 2)
        return pl.ds(pl.multiple_of(owner * block, block), block)

    kept = []

    def keep(part, pattern):
        copy = pltpu.make_async_copy(
            source(part, pattern),
            gathered_refs[part].at[place_of(pattern)],
            keep_sems.at[slot(part, pattern)],
        )
        copy.start()
        kept.append(copy)

    sequence = []
    for turn in range(len(near[0])):
        sequence += [(part, near[part][turn]) for part in range(parts)]
        sequence += [(part, near[part][turn] | 1) for part in range(parts)]
    stored = {}

    def fetch(number):
        part, pattern = sequence[number]
        copy = pltpu.make_async_copy(
            wide_refs[part].at[place_of(pattern)],
            wide_stage.at[number % 2],
            wide_sems.at[number % 2],
        )
        copy.start()
        return copy

    def multiply(number):
        part, pattern = sequence[number]
        turn = number % 2
        rows = source(part, pattern)
        for copy in stored.pop(number - 2, ()):
            copy.wait()
        if backward:
            stored_wide.pop(number).wait()

        @pl.loop(0, hidden // stride)
        def _(step):
            window = pl.ds(pl.multiple_of(step * stride, stride), stride)
            product = contract(rows[...], weight_ref[window], 1, 1)
            if backward:
                value = product * gelu_slope(wide_stage[turn, :, window])
            elif plain:
                value = product
            else:
                value = product + bias_ref[:, window]
                wide_stage[turn, :, window] = value
                value = gelu_tanh(value)
            low_stage[turn, :, window] = value.astype(LOW)

        if backward and number + 2 < len(sequence):
            stored_wide[number + 2] = fetch(number + 2)
        outgoing = [
            pltpu.make_async_copy(
                low_stage.at[turn], low_refs[part].at[place_of(pattern)], low_sems.at[turn]
            )
        ]
        if not backward and not plain:
            outgoing.append(
                pltpu.make_async_copy(
                    wide_stage.at[turn], wide_refs[part].at[place_of(pattern)], wide_sems.at[turn]
                )
            )
        for copy in outgoing:
            copy.start()
        stored[number] = outgoing

    stored_wide = {}
    if backward:
        for number in range(2):
            stored_wide[number] = fetch(number)
    for turn in range(len(bits)):
        for part in range(parts):
            pass_on(part, 0, orders[part][turn])
    for part in range(parts):
        pass_on(part, 0, 1)
        keep(part, 0)

    number = 0
    for turn in range(len(near[0])):
        if turn:
            for part in range(parts):
                pattern = near[part][turn]
                copies[part, pattern].wait_recv()
                highest = max(orders[part].index(bit) for bit in bits if pattern & bit)
                for bit in orders[part][highest + 1 :]:
                    pass_on(part, pattern, bit)
                pass_on(part, pattern, 1)
                keep(part, pattern)
        for part in range(parts):
            multiply(number)
            number += 1
        for part in range(parts):
            pattern = near[part][turn] | 1
            copies[part, pattern].wait_recv()
            keep(part, pattern)
            multiply(number)
            number += 1
    for outgoing in stored.values():
        for copy in outgoing:
            copy.wait()
    for copy in kept:
        copy.wait()
    for copy in copies.values():
        copy.wait_send()


def gather_product(blocks, weight, extra, collective_id):
    mode = "plain" if extra is None else "slope" if isinstance(extra, list) else "bias"
    parts = len(blocks)
    plane = lax.axis_size("dp")
    bits = [1 << k for k in range(1, plane.bit_length() - 1)]
    block, width = blocks[0].shape
    hidden = weight.shape[0]
    rows = plane * block
    vmem, anywhere = (
        pl.BlockSpec(memory_space=pltpu.VMEM),
        pl.BlockSpec(memory_space=pl.ANY),
    )
    gathered = jax.ShapeDtypeStruct((rows, width), LOW)
    wide = jax.ShapeDtypeStruct((rows, hidden), WIDE)
    low = jax.ShapeDtypeStruct((rows, hidden), LOW)
    outs = [gathered] * parts + ([wide] * parts if mode == "bias" else []) + [low] * parts
    extras = {"plain": [], "bias": [extra], "slope": extra}[mode]
    results = pl.pallas_call(
        functools.partial(gather_kernel, bits, parts, mode),
        out_shape=outs,
        in_specs=[vmem] * (parts + 1) + [anywhere if mode == "slope" else vmem] * len(extras),
        out_specs=[anywhere] * len(outs),
        scratch_shapes=[
            pltpu.VMEM((parts * plane, block, width), LOW),
            pltpu.VMEM((2, block, hidden), WIDE),
            pltpu.VMEM((2, block, hidden), LOW),
            pltpu.SemaphoreType.DMA((parts * plane,)),
            pltpu.SemaphoreType.DMA((parts * plane,)),
            pltpu.SemaphoreType.DMA((parts * plane,)),
            pltpu.SemaphoreType.DMA((2,)),
            pltpu.SemaphoreType.DMA((2,)),
        ],
        cost_estimate=pl.CostEstimate(
            flops=2 * parts * rows * hidden * width,
            bytes_accessed=16 * parts * rows * width,
            transcendentals=parts * rows * hidden,
        ),
        compiler_params=pltpu.CompilerParams(
            collective_id=collective_id, has_side_effects=True, vmem_limit_bytes=60 << 20
        ),
        name="gather_product",
    )(*blocks, weight, *extras)
    return [list(results[k : k + parts]) for k in range(0, len(outs), parts)]


def opening_kernel(bits, parts, depth, *refs):
    block_refs, piece_ref = refs[:parts], refs[parts]
    gathered_refs, line_ref = refs[parts + 1 : 2 * parts + 1], refs[2 * parts + 1]
    landed, held_line = refs[2 * parts + 2 : 2 * parts + 4]
    send_sems, recv_sems, keep_sems, line_send, line_recv, line_keep = refs[2 * parts + 4 :]
    rank, level = lax.axis_index("dp"), lax.axis_index("mp")
    block = block_refs[0].shape[0]

    def across(bit):
        return rank + bit - 2 * bit * (rank // bit % 2)

    partners = [1] + list(bits)
    plane = 1 << len(partners)
    barrier = pltpu.get_barrier_semaphore()
    for bit in partners:
        pl.semaphore_signal(
            barrier,
            inc=1,
            device_id={"dp": across(bit)},
            device_id_type=pl.DeviceIdType.MESH,
        )
    for shift in (1, depth - 1):
        pl.semaphore_signal(
            barrier,
            inc=1,
            device_id={"mp": (level + shift) % depth},
            device_id_type=pl.DeviceIdType.MESH,
        )
    pl.semaphore_wait(barrier, len(partners) + 2)

    def line_copy(up, step):
        shard = level - step if up else level + step
        number = step * 2 + (0 if up else 1)
        return pltpu.make_async_remote_copy(
            src_ref=held_line.at[shard] if step else piece_ref,
            dst_ref=held_line.at[shard],
            send_sem=line_send.at[number],
            recv_sem=line_recv.at[number],
            device_id={"mp": (level + (1 if up else depth - 1)) % depth},
            device_id_type=pl.DeviceIdType.MESH,
        )

    def sends(up, step):
        if up:
            return jnp.logical_and(level + 1 < depth, level >= step)
        return jnp.logical_and(level > 0, level + step < depth)

    def receives(up, step):
        return level > step if up else level + step + 1 < depth

    orders = [list(bits) if part % 2 == 0 else list(bits)[::-1] for part in range(parts)]
    near = [patterns_of(order) for order in orders]
    copies = {}

    def place_of(pattern):
        owner = rank
        for bit in partners:
            if pattern & bit:
                owner = owner + bit - 2 * bit * (rank // bit % 2)
        return pl.ds(pl.multiple_of(owner * block, block), block)

    def pass_on(part, pattern, bit):
        target = part * plane + (pattern | bit)
        copy = pltpu.make_async_remote_copy(
            src_ref=landed.at[part * plane + pattern] if pattern else block_refs[part],
            dst_ref=landed.at[target],
            send_sem=send_sems.at[target],
            recv_sem=recv_sems.at[target],
            device_id={"dp": across(bit)},
            device_id_type=pl.DeviceIdType.MESH,
        )
        copy.start()
        copies[part, pattern | bit] = copy

    def line_start(step):
        for up in (True, False):

            @pl.when(sends(up, step))
            def _():
                line_copy(up, step).start()

    line_start(0)
    for turn in range(len(bits)):
        for part in range(parts):
            pass_on(part, 0, orders[part][turn])
    kept = []

    def keep(part, pattern):
        number = part * plane + pattern
        copy = pltpu.make_async_copy(
            landed.at[number] if pattern else block_refs[part],
            gathered_refs[part].at[place_of(pattern)],
            keep_sems.at[number],
        )
        copy.start()
        kept.append(copy)

    def line_keep_copy(up, step):
        shard = level - step if up else level + step
        return pltpu.make_async_copy(
            held_line.at[shard] if step else piece_ref,
            line_ref.at[shard],
            line_keep.at[step * 2 - (0 if up else 1)],
        )

    for part in range(parts):
        pass_on(part, 0, 1)
        keep(part, 0)
    line_keep_copy(True, 0).start()
    for turn in range(1, max(len(near[0]), depth)):
        if turn < len(near[0]):
            for part in range(parts):
                pattern = near[part][turn]
                copies[part, pattern].wait_recv()
                highest = max(orders[part].index(bit) for bit in bits if pattern & bit)
                for bit in orders[part][highest + 1 :]:
                    pass_on(part, pattern, bit)
                pass_on(part, pattern, 1)
                keep(part, pattern)
        if turn < depth:
            for up in (True, False):

                @pl.when(receives(up, turn - 1))
                def _():
                    line_copy(up, turn - 1).wait_recv()
                    line_keep_copy(up, turn).start()

            if turn < depth - 1:
                line_start(turn)
    for part in range(parts):
        for pattern in near[part]:
            copies[part, pattern | 1].wait_recv()
            keep(part, pattern | 1)
    for copy in kept:
        copy.wait()
    for copy in copies.values():
        copy.wait_send()
    line_keep_copy(True, 0).wait()
    for step in range(depth - 1):
        for up in (True, False):

            @pl.when(receives(up, step))
            def _():
                line_keep_copy(up, step + 1).wait()

            @pl.when(sends(up, step))
            def _():
                line_copy(up, step).wait_send()


def opening_gather(blocks, piece, collective_id):
    parts = len(blocks)
    plane, depth = lax.axis_size("dp"), lax.axis_size("mp")
    bits = [1 << k for k in range(1, plane.bit_length() - 1)]
    block, width = blocks[0].shape
    anywhere = pl.BlockSpec(memory_space=pl.ANY)
    results = pl.pallas_call(
        functools.partial(opening_kernel, bits, parts, depth),
        out_shape=[jax.ShapeDtypeStruct((plane * block, width), LOW)] * parts
        + [jax.ShapeDtypeStruct((depth,) + piece.shape, LOW)],
        in_specs=[pl.BlockSpec(memory_space=pltpu.VMEM)] * (parts + 1),
        out_specs=[anywhere] * (parts + 1),
        scratch_shapes=[
            pltpu.VMEM((parts * plane, block, width), LOW),
            pltpu.VMEM((depth,) + piece.shape, LOW),
            pltpu.SemaphoreType.DMA((parts * plane,)),
            pltpu.SemaphoreType.DMA((parts * plane,)),
            pltpu.SemaphoreType.DMA((parts * plane,)),
            pltpu.SemaphoreType.DMA((2 * (depth - 1),)),
            pltpu.SemaphoreType.DMA((2 * (depth - 1),)),
            pltpu.SemaphoreType.DMA((2 * depth - 1,)),
        ],
        cost_estimate=pl.CostEstimate(
            flops=0, bytes_accessed=16 * parts * plane * block * width, transcendentals=0
        ),
        compiler_params=pltpu.CompilerParams(
            collective_id=collective_id, has_side_effects=True, vmem_limit_bytes=60 << 20
        ),
        name="opening_gather",
    )(*blocks, piece)
    return list(results[:parts]), results[parts]


def sum_over(axes, vector):
    for axis in axes:
        size = lax.axis_size(axis)
        step = 1
        while step < size:
            vector = vector + lax.ppermute(vector, axis, [(k, k ^ step) for k in range(size)])
            step *= 2
    return vector


def body(
    inputs,
    segment_ids,
    cotangent,
    query_weight,
    key_weight,
    value_weight,
    out_weight,
    up_weight,
    down_weight,
    query_bias,
    value_bias,
    out_bias,
    up_bias,
    down_bias,
    first_gain,
    first_shift,
    second_gain,
    second_shift,
):
    plane, depth = lax.axis_size("dp"), lax.axis_size("mp")
    rank, level = lax.axis_index("dp"), lax.axis_index("mp")
    parts, block, width = inputs.shape
    length = block * depth
    group = depth // parts
    seqs = plane // group
    rows = group * block
    hidden = up_bias.shape[0] // plane
    heads_in_block = query_weight.shape[1] // HEAD_DIM
    sharers = plane // heads_in_block
    heads = depth // sharers
    parity = level % parts

    def route(turn, back):
        pairs = []
        for i in range(plane):
            for j in range(depth):
                e = (j + turn) % parts
                source = i * depth + j
                target = (i - i % group + j // parts) * depth + parts * (i % group) + e
                pairs.append((target, source) if back else (source, target))
        return pairs

    def pick(options, index):
        return lax.dynamic_index_in_dim(jnp.stack(options), index % parts, 0, keepdims=False)

    def enter(array):
        arrived = [
            lax.ppermute(
                lax.dynamic_index_in_dim(array, (level + turn) % parts, 0, keepdims=False),
                ("dp", "mp"),
                route(turn, False),
            )
            for turn in range(parts)
        ]
        return [pick(arrived, parity - b + parts) for b in range(parts)]

    def leave_picks(blocks):
        return [pick(blocks, parity - turn + parts) for turn in range(parts)]

    def leave_sent(picks):
        return [
            lax.ppermute(picks[turn], ("dp", "mp"), route(turn, True)) for turn in range(parts)
        ]

    def leave_placed(arrived):
        return jnp.stack([pick(arrived, e - parity + parts) for e in range(parts)])

    def swap(array, bit):
        return lax.ppermute(array, "dp", [(k, k ^ bit) for k in range(plane)])

    bits = [1 << k for k in range(plane.bit_length() - 1)]

    sharing = [list(range(k, k + sharers)) for k in range(0, plane, sharers)]

    def share_out(array):
        if sharers == 1:
            return array
        return lax.all_to_all(
            array, "dp", split_axis=0, concat_axis=2, axis_index_groups=sharing, tiled=True
        )

    def share_back(array):
        if sharers == 1:
            return array
        return lax.all_to_all(
            array, "dp", split_axis=2, concat_axis=0, axis_index_groups=sharing, tiled=True
        )

    tokens = enter(inputs)
    attention_shards = jnp.stack([query_weight.T, key_weight.T, value_weight.T, out_weight])
    attention_shards = attention_shards.reshape(4, plane, -1, width // plane)
    attention_pieces = lax.all_to_all(
        attention_shards.transpose(1, 0, 2, 3).reshape(-1, width // plane),
        "dp",
        split_axis=0,
        concat_axis=1,
        tiled=True,
    )
    segments = segment_ids
    for bit in bits:
        other = swap(segments, bit)
        upper = rank // bit % 2 == 1
        segments = jnp.concatenate(
            [jnp.where(upper, other, segments), jnp.where(upper, segments, other)]
        )
    segments = lax.dynamic_index_in_dim(
        segments.reshape(seqs, depth, length), level, 1, keepdims=False
    )
    segments = segments.reshape(seqs, group, parts, block).transpose(0, 2, 1, 3)
    segment_rows = segments.reshape(seqs, parts, rows)
    segment_cols = segments.reshape(seqs, parts * rows, 1)
    tokens, segment_rows, segment_cols = together((tokens, segment_rows, segment_cols))
    forward_shards, attention_pieces = together(((up_weight.T, down_weight), attention_pieces))
    forward_pieces = lax.all_to_all(
        jnp.concatenate(
            [shard.reshape(plane, -1, width // plane) for shard in forward_shards], axis=1
        ).reshape(-1, width // plane),
        "dp",
        split_axis=0,
        concat_axis=1,
        tiled=True,
    )
    gathered_inputs, attention_line = opening_gather(tokens, attention_pieces, 7)
    attention_line, forward_pieces = together((attention_line, forward_pieces))
    up_piece, down_piece = jnp.split(forward_pieces, 2, axis=0)
    attention_full = share_out(attention_line.reshape(depth, 4, -1, width))
    attention_full = attention_full.transpose(1, 0, 2, 3).reshape(4, heads * HEAD_DIM, width)
    full_qkv = attention_full[:3].reshape(3 * heads * HEAD_DIM, width)
    full_out = attention_full[3]

    def own_heads(bias):
        table = bias.reshape(depth, heads_in_block, HEAD_DIM)
        return lax.dynamic_slice(
            table, (rank % sharers * heads, rank // sharers, 0), (heads, 1, HEAD_DIM)
        ).reshape(-1)

    qkv_bias = jnp.concatenate(
        [own_heads(query_bias), jnp.zeros((heads * HEAD_DIM,), WIDE), own_heads(value_bias)]
    )
    own_up = lax.dynamic_slice(
        up_bias.reshape(depth, plane, -1), (0, rank, 0), (depth, 1, hidden // depth)
    ).reshape(-1)

    every = range(parts)
    qkv = [
        (contract(gathered_inputs[b], full_qkv, 1, 1) + qkv_bias).astype(LOW) for b in every
    ]
    full_up = lax.all_gather(up_piece, "mp", axis=0, tiled=True)
    full_down = lax.all_gather(down_piece, "mp", axis=0, tiled=True)
    attended, lses = [], []
    for b in every:
        mixed, lse = attend_forward(b, qkv, segment_cols, segment_rows)
        attended.append(mixed)
        lses.append(lse)
    attn_sums = product_scatter(attended, full_out, 1)
    first = [
        norm_forward(tokens[b].astype(WIDE) + attn_sums[b] + out_bias, first_gain, first_shift)
        for b in every
    ]
    first_low = [first[b][0].astype(LOW) for b in every]
    first_low, full_up, cotangent = together((first_low, full_up, cotangent))
    tangents = enter(cotangent)
    gathered_first, up_proj, hiddens = gather_product(
        first_low, full_up, own_up.reshape(1, -1), 4
    )
    hiddens, tangents, full_down = together((hiddens, tangents, full_down))
    tangents = [array.astype(WIDE) for array in tangents]
    ffn_sums = product_scatter(hiddens, full_down, 2)
    second = [
        norm_forward(first[b][0] + ffn_sums[b] + down_bias, second_gain, second_shift)
        for b in every
    ]
    outputs = leave_placed(
        leave_sent(leave_picks([second[b][0].astype(LOW) for b in every]))
    )

    def share_attention(term):
        return share_back(term.reshape(-1, heads, HEAD_DIM, width).transpose(1, 0, 2, 3))

    def reduce_attention(term):
        return lax.psum_scatter(share_attention(term), "mp", scatter_dimension=0, tiled=True)[0]

    def reduce_forward(term):
        return lax.psum_scatter(term, "mp", scatter_dimension=0, tiled=True)

    def owner_exchange(term):
        return lax.all_to_all(
            term.reshape(-1, width), "dp", split_axis=1, concat_axis=0, tiled=True
        )

    def low_sum(terms):
        return sum(terms).astype(LOW)

    def total(arrays):
        return sum(jnp.sum(array.astype(WIDE), axis=0) for array in arrays)

    grad_second_gain = total([tangents[b] * second[b][1] for b in every])
    grad_second_shift = total(tangents)
    grad_two = [
        norm_backward(tangents[b], second[b][1], second[b][2], second_gain) for b in every
    ]
    grad_ffn = [array.astype(LOW) for array in grad_two]
    grad_down_bias = total(grad_ffn)
    gathered_ffn, grad_upper = gather_product(grad_ffn, full_down, up_proj, 5)
    gathered_ffn, grad_upper, outputs = together((gathered_ffn, grad_upper, outputs))
    grad_up_bias = total(grad_upper)
    back_sums, term_up = product_scatter(grad_upper, full_up, 8, gathered_first)
    term_down = low_sum(contract(hiddens[b], gathered_ffn[b], 0, 0) for b in every)
    grad_first = [grad_two[b] + back_sums[b] for b in every]
    grad_first_gain = total([grad_first[b] * first[b][1] for b in every])
    grad_first_shift = total(grad_first)
    grad_resid = [
        norm_backward(grad_first[b], first[b][1], first[b][2], first_gain) for b in every
    ]
    grad_branch = [array.astype(LOW) for array in grad_resid]
    reduced_down = reduce_forward(term_down)
    grad_branch, reduced_down = together((grad_branch, reduced_down))
    grad_out_bias = total(grad_branch)
    gathered_branch, grad_mixed = gather_product(grad_branch, full_out, None, 6)
    spread_up = lax.dynamic_update_slice(
        jnp.zeros((depth, plane, hidden // depth), WIDE),
        grad_up_bias.reshape(depth, 1, -1),
        (0, rank, 0),
    ).reshape(-1)
    owned_down = owner_exchange(reduced_down)
    reduced_up = reduce_forward(term_up)
    grad_mixed = [
        array.reshape(seqs * rows, heads * HEAD_DIM)
        for array in grad_mixed
    ]
    grad_qkv, grad_qkv_bias = attend_backward(qkv, grad_mixed, lses, segment_cols, segment_rows)

    def spread_heads(piece):
        table = jnp.zeros((depth, heads_in_block, HEAD_DIM), WIDE)
        return lax.dynamic_update_slice(
            table,
            piece.reshape(heads, 1, HEAD_DIM),
            (rank % sharers * heads, rank // sharers, 0),
        ).reshape(-1)

    spread = heads * HEAD_DIM
    vectors = jnp.concatenate(
        [
            spread_heads(grad_qkv_bias[:spread]),
            spread_heads(grad_qkv_bias[2 * spread :]),
            grad_out_bias,
            grad_down_bias,
            grad_first_gain,
            grad_first_shift,
            grad_second_gain,
            grad_second_shift,
            spread_up,
        ]
    )
    vectors = sum_over(("mp",), vectors.reshape(-1, HEAD_DIM))
    reduced_out = reduce_attention(
        low_sum(contract(attended[b], gathered_branch[b], 0, 0) for b in every)
    )
    term_qkv = low_sum(contract(grad_qkv[b], gathered_inputs[b], 0, 0) for b in every)
    term_qkv, reduced_up = together((term_qkv, reduced_up))
    shared_qkv = share_attention(term_qkv)
    owned_up = owner_exchange(reduced_up)
    grad_qkv, shared_qkv, vectors = together((grad_qkv, shared_qkv, vectors))
    input_sums = product_scatter(grad_qkv, full_qkv, 3)
    reduced_qkv = lax.psum_scatter(shared_qkv, "mp", scatter_dimension=0, tiled=True)[0]
    grad_low = [(grad_resid[b] + input_sums[b]).astype(LOW) for b in every]
    leaving = leave_sent(leave_picks(grad_low))
    vectors = sum_over(("dp",), vectors).reshape(-1)
    grad_inputs = leave_placed(leaving).astype(WIDE)

    owned_out = owner_exchange(reduced_out)
    owned_qkv = owner_exchange(reduced_qkv)
    owned_qkv = owned_qkv.reshape(plane, 3, -1, width // plane).transpose(1, 0, 2, 3)
    owned_qkv = owned_qkv.reshape(3, -1, width // plane)

    narrow = vectors[: 8 * width].reshape(8, width)
    return (
        outputs,
        grad_inputs,
        owned_qkv[0].T.astype(WIDE),
        owned_qkv[1].T.astype(WIDE),
        owned_qkv[2].T.astype(WIDE),
        owned_out.astype(WIDE),
        owned_up.T.astype(WIDE),
        owned_down.astype(WIDE),
        narrow[0],
        narrow[1],
        narrow[2],
        vectors[8 * width :],
        narrow[3],
        narrow[4],
        narrow[5],
        narrow[6],
        narrow[7],
    )


def solution(mesh):
    tokens = P("dp", "mp", None)
    by_rows, by_columns, whole = P("dp", "mp"), P("mp", "dp"), P()
    in_specs = (
        (tokens, P("dp", None), tokens)
        + (by_rows,) * 3
        + (by_columns, by_rows, by_columns)
        + (whole,) * 9
    )
    out_specs = (
        (tokens, tokens) + (by_rows,) * 3 + (by_columns, by_rows, by_columns) + (whole,) * 9
    )
    return jax.shard_map(body, mesh=mesh, in_specs=in_specs, out_specs=out_specs, check_vma=False)
```
